32 devices in a mesh: groups: 2 (over x), hid: 16 (over z, y, core).
Axes of the slice: x: 2, y: 2, z: 4, core: 2. Of those that a mesh axis runs over, the one named last changes fastest.
Arguments:
- tokens: bfloat16 [256, 8192], P(('groups', 'hid')), parts along dimension 0, may hold values from -6 to 6
- norm_gain: float32 [8192], replicated, may hold values from 0.1 to 1.9
- gate_weight: bfloat16 [8192, 16384], P(None, 'hid'), may hold values from -0.0625 to 0.0625
- up_weight: bfloat16 [8192, 16384], P(None, 'hid'), may hold values from -0.0625 to 0.0625
- down_weight: bfloat16 [16384, 8192], P('hid'), may hold values from -0.046875 to 0.046875
- clip_scale: float32 [16384], P('hid'), may hold values from 0.002 to 0.02
Outputs:
- mixed: bfloat16 [256, 8192], P(('groups', 'hid')), parts along dimension 0
The draws below stay inside these ranges and needn't reach their ends.
There are 2 independent parts, one for each index of `groups`. The reference program is written for one: setup_inputs(seed, part) draws one part's arguments, and reference() takes and returns one part's arrays. A program takes and returns all parts, laid end to end along the dimension named above; an argument that names none is the same for every part. Nothing has to cross between parts.
All inputs are finite; a program needn't handle non-finite values.
Results may differ from the reference program's by a relative error of at most 0.006.
Values may be sent and summed in bfloat16 or wider, within the bound.
A program may use at most 128 MiB of HBM per device.

```python
import math
import jax
import jax.numpy as jnp
from jax import lax

D = 8192
FF = 16384
BLOCK = 256
TOKENS = 128


def block_scale(own_key, extent, split, smallest, top_value):
    level = 1.0
    for axis_at, blocks in split:
        draws = jax.random.uniform(jax.random.fold_in(jax.random.fold_in(own_key, 6), axis_at), (blocks,), jnp.float32, smallest / len(split), top_value / len(split))
        level = level * jnp.repeat(jnp.exp(draws), extent[axis_at] // blocks).reshape((-1,) + (1,) * (len(extent) - 1 - axis_at))
    return level


def scatter_about(rng, shape, width, reach, split=(), kind=jnp.bfloat16):
    array = jax.random.normal(rng, shape, jnp.float32) * width
    if len(split) > 0:
        array = block_scale(rng, shape, split, -0.22, 0.18) * array
    return jnp.clip(array, min=-reach, max=reach).astype(kind)


def setup_inputs(seed: int = 0, part: int = 0) -> dict:
    streams_of = jax.random.split(jax.random.key(seed), 7)
    part_splits = jax.random.split(jax.random.fold_in(streams_of[6], part), 7)
    tokens = scatter_about(part_splits[0], (TOKENS, D), 1.0, 6.0, ((0, 16),))
    norm_gain = jnp.clip(1.0 + 0.18 * jax.random.normal(streams_of[1], (D,), jnp.float32), 0.1, 1.9)
    gate_weight = scatter_about(streams_of[2], (D, FF), D ** -0.5, 0.0625, ((1, 16),))
    up_weight = scatter_about(streams_of[3], (D, FF), D ** -0.5, 0.0625, ((1, 16),))
    down_weight = scatter_about(streams_of[4], (FF, D), FF ** -0.5, 0.046875, ((0, 16),))
    clip_scale = jnp.clip(jnp.exp(math.log(0.02) - 2.30258502 * jax.random.uniform(streams_of[5], (FF,), jnp.float32) ** block_scale(streams_of[5], (FF,), ((0, 16),), -0.2, 0.2)), 0.002, 0.02)
    return dict(tokens=tokens, norm_gain=norm_gain, gate_weight=gate_weight, up_weight=up_weight, down_weight=down_weight, clip_scale=clip_scale)


def hadamard(count):
    rows = jnp.arange(count, dtype=jnp.int32)[:, None]
    cols = jnp.arange(count, dtype=jnp.int32)[None, :]
    both = rows & cols
    parity = jnp.zeros((count, count), jnp.int32)
    for place in range(max(count.bit_length(), 1)):
        parity = parity + (both >> place & 1)
    return jnp.where(parity % 2 == 0, 1.0, -1.0).astype(jnp.float32)

def reference(tokens, norm_gain, gate_weight, up_weight, down_weight, clip_scale):
    values = tokens.astype(jnp.float32)
    inverse = lax.rsqrt(lax.optimization_barrier(jnp.mean(values * values, axis=-1, keepdims=True)) + 1e-05)
    normed = (values * inverse * norm_gain).astype(jnp.bfloat16)
    gate = jnp.dot(normed, gate_weight, preferred_element_type=jnp.float32)
    up = jnp.dot(normed, up_weight, preferred_element_type=jnp.float32)
    hidden = jax.nn.silu(gate) * up
    blocks = FF // BLOCK
    shaped = hidden.reshape(TOKENS, blocks, BLOCK)
    shaped = jnp.einsum('tbc,cd->tbd', shaped, hadamard(BLOCK), precision=lax.Precision.HIGHEST)
    shaped = jnp.einsum('tbc,be->tec', shaped, hadamard(blocks), precision=lax.Precision.HIGHEST)
    rotated = shaped.reshape(TOKENS, FF) / jnp.sqrt(jnp.float32(FF))
    limit = 127.0 * clip_scale
    clipped = jnp.clip(rotated, -limit, limit).astype(jnp.bfloat16)
    result = values + jnp.dot(clipped, down_weight, preferred_element_type=jnp.float32)
    return result.astype(jnp.bfloat16)
```

```python
import functools
import math

import jax
import jax.numpy as jnp
from jax import lax
from jax.experimental import pallas as pl
from jax.experimental.pallas import tpu as pltpu
from jax.sharding import PartitionSpec as P

BLOCK = 256
STEPS = 8
OUT_STEPS = 8
AHEAD = 5
LAG = ((2, 10), (8, 13), (10, 15), (16, 18))
MESH = pl.DeviceIdType.MESH
BF = jnp.bfloat16
F32 = jnp.float32


def walsh(parts):
    parts = list(parts)
    half = 1
    while half < len(parts):
        for at in range(len(parts)):
            if at & half == 0:
                low, high = parts[at], parts[at + half]
                parts[at], parts[at + half] = low + high, low - high
        half *= 2
    return parts


def kernel(n, tok, gain, wg, wu, wd, clip, out,
           x, vg, vu, vd, gate, up, table, hs, hr, bs, br, y,
           own, cs, cr, ys, yr, zs, zr, pr,
           wsem, dsem, ag_send, core_send, relay_send, z_recv, y_recv, c_recv,
           a_send, b_send, a_recv, b_recv, rs_send,
           rc_recv, ry_recv, rz_recv, rp_recv):
    me = lax.axis_index("hid")
    line, chips = n // 4, n // 2
    a, b, c = me // 4, (me // 2) % 2, me % 2
    k = me // 2
    odd = a % 2
    mate = a + 1 - 2 * odd
    rows, width = tok.shape
    local = vg.shape[1]
    span = width // STEPS
    ospan = out.shape[1] // OUT_STEPS
    core_peer = me + 1 - 2 * c
    y_peer = (a * 2 + 1 - b) * 2 + c

    def device(a_at):
        return (a_at * 2 + b) * 2 + c

    def other(nth):
        low = nth + (nth >= a).astype(jnp.int32)
        high = line - 1 - nth - ((line - 1 - nth) <= a).astype(jnp.int32)
        return jnp.where(a < line // 2, low, high)

    def outward(a_at):
        return jnp.where(odd == 0, a_at > a, a_at < a)

    def inward(a_at):
        return jnp.where(odd == 0, a_at < a, a_at > a)

    def send(src, dst, ssem, rsem, to):
        pltpu.make_async_remote_copy(
            src_ref=src, dst_ref=dst, send_sem=ssem, recv_sem=rsem,
            device_id={"hid": to}, device_id_type=MESH).start()

    def settle(ref, sem):
        pltpu.make_async_copy(ref, ref, sem).wait()

    barrier = pltpu.get_barrier_semaphore()
    for shift in range(1, n):
        pl.semaphore_signal(barrier, inc=1, device_id={"hid": lax.rem(me + shift, n)}, device_id_type=MESH)

    weight_copies = []
    for s in range(STEPS):
        part = pl.ds(s * span, span)
        weight_copies.append((
            pltpu.make_async_copy(wg.at[part, :], vg.at[part, :], wsem.at[0, s]),
            pltpu.make_async_copy(wu.at[part, :], vu.at[part, :], wsem.at[1, s])))
        for copy in weight_copies[-1]:
            copy.start()
    down_copies = []
    for t in range(OUT_STEPS):
        part = pl.ds(t * ospan, ospan)
        down_copies.append(pltpu.make_async_copy(wd.at[:, part], vd.at[:, part], dsem.at[t]))
        down_copies[-1].start()

    values = tok[...].astype(F32)
    inverse = lax.rsqrt(jnp.mean(values * values, axis=-1, keepdims=True) + 1e-05)
    x[c, k] = (values * inverse * gain[...]).astype(BF)

    at_row = lax.broadcasted_iota(jnp.int32, (BLOCK, BLOCK), 0)
    at_col = lax.broadcasted_iota(jnp.int32, (BLOCK, BLOCK), 1)
    bits = at_row & at_col
    folded = bits
    for place in range(1, (BLOCK - 1).bit_length()):
        folded = folded ^ (bits >> place)
    table[...] = (1 - 2 * (folded & 1)).astype(F32).astype(BF)

    with jax.named_scope("barrier"):
        pl.semaphore_wait(barrier, n - 1)

    def block(a_at, b_at, s):
        return x.at[c, a_at * 2 + b_at, :, pl.ds(s * span, span)]

    def begin_line(s):
        mine = block(a, b, s)
        for step in range(1, line // 2):
            pair = lax.rem(a // 2 + step, line // 2)
            near = 2 * pair + (pair < a // 2).astype(jnp.int32)
            send(mine, mine, ag_send, z_recv.at[s, a], device(near))
        send(mine, mine, ag_send, z_recv.at[s, a], device(mate))

    def begin_rows(s):
        mine = block(a, b, s)
        send(mine, mine, ag_send, y_recv.at[s, a], y_peer)
        send(mine, mine, core_send, c_recv.at[s], core_peer)

    for s in range(STEPS):
        if s < AHEAD:
            begin_line(s)
        begin_rows(s)

    def relay_line(s):
        for nth in range(line - 1):
            src = other(nth)
            got = block(src, b, s)
            settle(got, z_recv.at[s, src])

            @pl.when(inward(src))
            def _():
                send(got, got, relay_send, z_recv.at[s, src], device(mate))
            send(got, got, ag_send, y_recv.at[s, src], y_peer)
            send(got, got, core_send, c_recv.at[s], core_peer)

    def relay_rows(s):
        for nth in range(line):
            src = a if nth == 0 else other(nth - 1)
            got = block(src, 1 - b, s)
            settle(got, y_recv.at[s, src])
            send(got, got, core_send, c_recv.at[s], core_peer)

    def project(s):
        part = pl.ds(s * span, span)
        with jax.named_scope("pwait"):
            settle(x.at[1 - c, :, :, part], c_recv.at[s])
        with jax.named_scope("wwait"):
            for copy in weight_copies[s]:
                copy.wait()
        left = x[:, :, :, part].reshape(n * rows, span)
        for acc, weight in ((gate, vg), (up, vu)):
            term = jnp.dot(left, weight[part, :], preferred_element_type=F32)
            acc[...] = term if s == 0 else acc[...] + term

    for s in range(STEPS + 3):
        if s < STEPS:
            with jax.named_scope(f"relay_line{s}"):
                relay_line(s)
        if s + AHEAD < STEPS:
            begin_line(s + AHEAD)
        if 0 <= s - 2 < STEPS:
            with jax.named_scope(f"relay_rows{s-2}"):
                relay_rows(s - 2)
        if 0 <= s - 3 < STEPS:
            with jax.named_scope(f"project{s-3}"):
                project(s - 3)

    with jax.named_scope("swiglu"):
        for at in range(local // BLOCK):
            tile = pl.ds(at * BLOCK, BLOCK)
            value = gate[:, tile]
            hidden = value / (1.0 + jnp.exp(-value)) * up[:, tile]
            gate[:, tile] = jnp.dot(hidden.astype(BF), table[...], preferred_element_type=F32)
    with jax.named_scope("walsh0"):
        for h in range(2):
            for q in range(chips):
                values = gate[pl.ds((h * chips + q) * rows, rows), :]
                turned = walsh([values[:, at * BLOCK:(at + 1) * BLOCK] for at in range(local // BLOCK)])
                hs[h, q] = (turned[0] if len(turned) == 1 else jnp.concatenate(turned, axis=1)).astype(BF)

    with jax.named_scope("exch0"):
        send(hs.at[1 - c, k], hr.at[me], a_send, a_recv, core_peer)
        for h in range(2):
            for shift in range(1, chips):
                q = lax.rem(k + shift, chips)
                send(hs.at[h, q], hr.at[me], a_send, a_recv, q * 2 + h)
        keep = pltpu.make_async_copy(hs.at[c, k], hr.at[me], a_recv)
        keep.start()
        settle(hr, a_recv)
    factor = 1.0 / math.sqrt(n * local)
    lanes = 128
    with jax.named_scope("walsh1"):
        for j in range(local // lanes):
            tile = pl.ds(j * lanes, lanes)
            turned = walsh([hr[d, :, tile].astype(F32) for d in range(n)])
            for d in range(n):
                bs[d, :, tile] = (turned[d] * factor).astype(BF)
    with jax.named_scope("exch1"):
        for shift in range(1, n):
            to = lax.rem(me + shift, n)
            send(bs.at[to], br.at[c, k], b_send, b_recv.at[c], to)
        pltpu.make_async_copy(bs.at[me], br.at[c, k], b_recv.at[c]).start()

    limit = 127.0 * clip[...]

    def clipped(h):
        with jax.named_scope(f"cwait{h}"):
            settle(br.at[h], b_recv.at[h])
        for q in range(chips // 2):
            values = jnp.concatenate([br[h, 2 * q].astype(F32), br[h, 2 * q + 1].astype(F32)], axis=0)
            y[h, pl.ds(2 * q * rows, 2 * rows), :] = jnp.clip(values, -limit, limit).astype(BF)

    def down(h, t):
        part = pl.ds(pl.multiple_of(t * ospan, ospan), ospan)
        if h == 0:
            pltpu.make_async_copy(wd.at[:, part], vd.at[:, part], dsem.at[t]).wait()
        own[h, t] = jnp.dot(y[h], vd[:, part], preferred_element_type=F32).reshape(chips, rows, ospan)

        @pl.when(c != h)
        def _():
            cs[t] = own[h, t].astype(BF)
            send(cs.at[t], cr.at[t], rs_send.at[0], rc_recv.at[t], core_peer)

    def over_rows(t):
        settle(cr.at[t], rc_recv.at[t])
        for at in range(line):
            ys[t, at] = (own[c, t, at * 2 + 1 - b] + cr[t, at * 2 + 1 - b].astype(F32)).astype(BF)
        send(ys.at[t], yr.at[t], rs_send.at[1], ry_recv.at[t], y_peer)

    def column(t, at):
        return own[c, t, at * 2 + b] + cr[t, at * 2 + b].astype(F32) + yr[t, at].astype(F32)

    def to_mate(t):
        settle(yr.at[t], ry_recv.at[t])
        for at in range(line):
            @pl.when(outward(at))
            def _():
                zs[t, at] = column(t, at).astype(BF)
                send(zs.at[t, at], zr.at[t, at], rs_send.at[2], rz_recv.at[t, at], device(mate))

    def to_line(t):
        for at in range(line):
            @pl.when(inward(at))
            def _():
                settle(zr.at[t, at], rz_recv.at[t, at])
                zs[t, at] = (column(t, at) + zr[t, at].astype(F32)).astype(BF)
                send(zs.at[t, at], pr.at[t, a // 2], rs_send.at[2], rp_recv.at[t, a // 2], device(at))

    def finish(t):
        settle(zr.at[t, a], rz_recv.at[t, a])
        values = column(t, a) + zr[t, a].astype(F32)
        for step in range(1, line // 2):
            pair = lax.rem(a // 2 + step, line // 2)
            settle(pr.at[t, pair], rp_recv.at[t, pair])
            values = values + pr[t, pair].astype(F32)
        part = pl.ds(pl.multiple_of(t * ospan, ospan), ospan)
        out[:, part] = (tok[:, part].astype(F32) + values).astype(out.dtype)

    def stages(u):
        for (first, last), stage in zip(LAG, (over_rows, to_mate, to_line, finish)):
            t = u - first - (last - first) * c

            @pl.when((t >= 0) & (t < OUT_STEPS))
            def _():
                with jax.named_scope(stage.__name__):
                    stage(t)

    def run(h, start, count):
        @pl.loop(0, count)
        def _(i):
            if h is not None:
                with jax.named_scope("down"):
                    down(h, i)
            stages(start + i)

    clipped(0)
    run(0, 0, OUT_STEPS)
    clipped(1)
    run(1, OUT_STEPS, OUT_STEPS)
    run(None, 2 * OUT_STEPS, LAG[-1][1] - OUT_STEPS)

    with jax.named_scope("drain"):
        for copies in range(1, line):
            @pl.when(jnp.where(odd == 0, a, line - 1 - a) == copies)
            def _():
                settle(x.at[0, pl.ds(0, copies)], relay_send)
        settle(x.at[0], core_send)
        settle(x.at[0, pl.ds(0, line + line // 2)], ag_send)
        settle(hr.at[pl.ds(0, n - 1)], a_send)
        settle(hr.at[pl.ds(0, n - 1)], b_send)
        settle(cs, rs_send.at[0])
        settle(ys, rs_send.at[1])
        settle(zs.at[:, pl.ds(0, line - 1)], rs_send.at[2])


def layer(n, tokens, norm_gain, gate_weight, up_weight, down_weight, clip_scale):
    rows, width = tokens.shape
    local = gate_weight.shape[1]
    outs = down_weight.shape[1]
    line, chips = n // 4, n // 2
    total = n * rows
    ospan = outs // OUT_STEPS
    vmem = pl.BlockSpec(memory_space=pltpu.VMEM)
    hbm = pl.BlockSpec(memory_space=pl.ANY)
    dma = pltpu.SemaphoreType.DMA
    return pl.pallas_call(
        functools.partial(kernel, n),
        out_shape=jax.ShapeDtypeStruct((rows, outs), BF),
        in_specs=[vmem, vmem, hbm, hbm, hbm, vmem],
        out_specs=vmem,
        scratch_shapes=[
            pltpu.VMEM((2, chips, rows, width), BF),
            pltpu.VMEM((width, local), BF),
            pltpu.VMEM((width, local), BF),
            pltpu.VMEM((local, outs), BF),
            pltpu.VMEM((total, local), F32),
            pltpu.VMEM((total, local), F32),
            pltpu.VMEM((BLOCK, BLOCK), BF),
            pltpu.VMEM((2, chips, rows, local), BF),
            pltpu.VMEM((n, rows, local), BF),
            pltpu.VMEM((n, rows, local), BF),
            pltpu.VMEM((2, chips, rows, local), BF),
            pltpu.VMEM((2, chips * rows, local), BF),
            pltpu.VMEM((2, OUT_STEPS, chips, rows, ospan), F32),
            pltpu.VMEM((OUT_STEPS, chips, rows, ospan), BF),
            pltpu.VMEM((OUT_STEPS, chips, rows, ospan), BF),
            pltpu.VMEM((OUT_STEPS, line, rows, ospan), BF),
            pltpu.VMEM((OUT_STEPS, line, rows, ospan), BF),
            pltpu.VMEM((OUT_STEPS, line, rows, ospan), BF),
            pltpu.VMEM((OUT_STEPS, line, rows, ospan), BF),
            pltpu.VMEM((OUT_STEPS, line // 2, rows, ospan), BF),
            dma((2, STEPS)), dma((OUT_STEPS,)), dma(()), dma(()), dma(()),
            dma((STEPS, line)), dma((STEPS, line)), dma((STEPS,)),
            dma(()), dma(()), dma(()), dma((2,)), dma((3,)),
            dma((OUT_STEPS,)), dma((OUT_STEPS,)), dma((OUT_STEPS, line)), dma((OUT_STEPS, line // 2)),
        ],
        compiler_params=pltpu.CompilerParams(
            collective_id=0, has_side_effects=True, vmem_limit_bytes=67043328),
    )(tokens, norm_gain.reshape(1, -1), gate_weight, up_weight, down_weight, clip_scale.reshape(1, -1))


def solution(mesh):
    in_specs = (
        P(("groups", "hid"), None),
        P(),
        P(None, "hid"),
        P(None, "hid"),
        P("hid", None),
        P("hid"),
    )
    return jax.shard_map(
        functools.partial(layer, mesh.shape["hid"]), mesh=mesh, in_specs=in_specs,
        out_specs=P(("groups", "hid"), None), check_vma=False)
```

```python
import functools
import math

import jax
import jax.numpy as jnp
from jax import lax
from jax.experimental import pallas as pl
from jax.experimental.pallas import tpu as pltpu
from jax.sharding import PartitionSpec as P

BLOCK = 256
STEPS = 8
OUT_STEPS = 8
AHEAD = 8
LAG = ((2, 10), (10, 18), (12, 20), (20, 28))
LATE = 18
MESH = pl.DeviceIdType.MESH
BF = jnp.bfloat16
F32 = jnp.float32


def walsh(parts):
    parts = list(parts)
    half = 1
    while half < len(parts):
        for at in range(len(parts)):
            if at & half == 0:
                low, high = parts[at], parts[at + half]
                parts[at], parts[at + half] = low + high, low - high
        half *= 2
    return parts


def kernel(n, tok, gain, wg, wu, wd, clip, out,
           x, vg, vu, vd, gate, up, table, hs, hr, bs, br, y,
           own, cs, cr, ys, yr, zs, zr, pr,
           wsem, dsem, ag_send, core_send, relay_send, z_recv, y_recv, c_recv,
           a_send, b_send, a_recv, b_recv, rs_send,
           rc_recv, ry_recv, rz_recv, rp_recv):
    me = lax.axis_index("hid")
    line, chips = n // 4, n // 2
    a, b, c = me // 4, (me // 2) % 2, me % 2
    k = me // 2
    odd = a % 2
    mate = a + 1 - 2 * odd
    rows, width = tok.shape
    local = vg.shape[1]
    span = width // STEPS
    ospan = out.shape[1] // OUT_STEPS
    core_peer = me + 1 - 2 * c
    y_peer = (a * 2 + 1 - b) * 2 + c

    def device(a_at):
        return (a_at * 2 + b) * 2 + c

    def other(nth):
        down = jnp.where(a == 0, 1 + nth, lax.rem(a + line - 1 - nth, line))
        up = jnp.where(a == line - 1, line - 2 - nth, lax.rem(a + 1 + nth, line))
        return jnp.where(odd == 0, down, up)

    def outward(a_at):
        return jnp.where(odd == 0, a_at > a, a_at < a)

    def inward(a_at):
        return jnp.where(odd == 0, a_at < a, a_at > a)

    def send(src, dst, ssem, rsem, to):
        pltpu.make_async_remote_copy(
            src_ref=src, dst_ref=dst, send_sem=ssem, recv_sem=rsem,
            device_id={"hid": to}, device_id_type=MESH).start()

    def settle(ref, sem):
        pltpu.make_async_copy(ref, ref, sem).wait()

    barrier = pltpu.get_barrier_semaphore()

    def greet(to):
        pl.semaphore_signal(barrier, inc=1, device_id={"hid": to}, device_id_type=MESH)

    greet(core_peer)
    greet(y_peer)
    greet(device(mate))
    for at in range(line):
        @pl.when(inward(at))
        def _():
            greet(device(at))

    weight_copies = []
    for s in range(STEPS):
        part = pl.ds(s * span, span)
        weight_copies.append((
            pltpu.make_async_copy(wg.at[part, :], vg.at[part, :], wsem.at[0, s]),
            pltpu.make_async_copy(wu.at[part, :], vu.at[part, :], wsem.at[1, s])))
        for copy in weight_copies[-1]:
            copy.start()
    down_copies = []
    for t in range(OUT_STEPS):
        part = pl.ds(t * ospan, ospan)
        down_copies.append(pltpu.make_async_copy(wd.at[:, part], vd.at[:, part], dsem.at[t]))
        down_copies[-1].start()

    values = tok[...].astype(F32)
    inverse = lax.rsqrt(jnp.mean(values * values, axis=-1, keepdims=True) + 1e-05)
    x[c, k] = (values * inverse * gain[...]).astype(BF)

    at_row = lax.broadcasted_iota(jnp.int32, (BLOCK, BLOCK), 0)
    at_col = lax.broadcasted_iota(jnp.int32, (BLOCK, BLOCK), 1)
    bits = at_row & at_col
    folded = bits
    for place in range(1, (BLOCK - 1).bit_length()):
        folded = folded ^ (bits >> place)
    table[...] = (1 - 2 * (folded & 1)).astype(F32).astype(BF)

    with jax.named_scope("barrier"):
        pl.semaphore_wait(barrier, 2 + line // 2)

    def block(a_at, b_at, s):
        return x.at[c, a_at * 2 + b_at, :, pl.ds(s * span, span)]

    def begin_line(s):
        mine = block(a, b, s)
        for step in range(1, line // 2):
            pair = lax.rem(a // 2 + step, line // 2)
            near = 2 * pair + (pair < a // 2).astype(jnp.int32)
            send(mine, mine, ag_send, z_recv.at[s, a], device(near))
        send(mine, mine, ag_send, z_recv.at[s, a], device(mate))

    def begin_rows(s):
        mine = block(a, b, s)
        send(mine, mine, ag_send, y_recv.at[s, a], y_peer)
        send(mine, mine, core_send, c_recv.at[s], core_peer)

    for s in range(STEPS):
        if s < AHEAD:
            begin_line(s)
        begin_rows(s)

    def relay_line(s, first, last):
        for nth in range(first, last):
            src = other(nth)
            got = block(src, b, s)
            settle(got, z_recv.at[s, src])

            @pl.when(inward(src))
            def _():
                send(got, got, relay_send, z_recv.at[s, src], device(mate))
            send(got, got, ag_send, y_recv.at[s, src], y_peer)
            send(got, got, core_send, c_recv.at[s], core_peer)

    def relay_rows(s):
        for nth in range(line):
            src = a if nth == 0 else other(nth - 1)
            got = block(src, 1 - b, s)
            settle(got, y_recv.at[s, src])
            send(got, got, core_send, c_recv.at[s], core_peer)

    def project(s):
        part = pl.ds(s * span, span)
        with jax.named_scope("pwait"):
            settle(x.at[1 - c, :, :, part], c_recv.at[s])
        with jax.named_scope("wwait"):
            for copy in weight_copies[s]:
                copy.wait()
        left = x[:, :, :, part].reshape(n * rows, span)
        for acc, weight in ((gate, vg), (up, vu)):
            term = jnp.dot(left, weight[part, :], preferred_element_type=F32)
            acc[...] = term if s == 0 else acc[...] + term

    outer = (a == 0) | (a == line - 1)

    @pl.when(outer)
    def _():
        for s in range(STEPS):
            with jax.named_scope(f"relay_first{s}"):
                relay_line(s, 0, 1)

    for s in range(STEPS + 5):
        if s < STEPS:
            with jax.named_scope(f"relay_line{s}"):
                @pl.when(jnp.logical_not(outer))
                def _():
                    relay_line(s, 0, 1)
                relay_line(s, 1, line - 1)
        if 0 <= s - 4 < STEPS:
            with jax.named_scope(f"relay_rows{s-4}"):
                relay_rows(s - 4)
        if 0 <= s - 5 < STEPS:
            with jax.named_scope(f"project{s-5}"):
                project(s - 5)

    with jax.named_scope("swiglu"):
        for at in range(local // BLOCK):
            tile = pl.ds(at * BLOCK, BLOCK)
            value = gate[:, tile]
            hidden = value / (1.0 + jnp.exp(-value)) * up[:, tile]
            gate[:, tile] = jnp.dot(hidden.astype(BF), table[...], preferred_element_type=F32)
    with jax.named_scope("walsh0"):
        for h in range(2):
            for q in range(chips):
                values = gate[pl.ds((h * chips + q) * rows, rows), :]
                turned = walsh([values[:, at * BLOCK:(at + 1) * BLOCK] for at in range(local // BLOCK)])
                hs[h, q] = (turned[0] if len(turned) == 1 else jnp.concatenate(turned, axis=1)).astype(BF)

    with jax.named_scope("exch0"):
        send(hs.at[1 - c, k], hr.at[me], a_send, a_recv, core_peer)
        for h in range(2):
            for shift in range(1, chips):
                q = lax.rem(k + shift, chips)
                send(hs.at[h, q], hr.at[me], a_send, a_recv, q * 2 + h)
        keep = pltpu.make_async_copy(hs.at[c, k], hr.at[me], a_recv)
        keep.start()
        settle(hr, a_recv)
    factor = 1.0 / math.sqrt(n * local)
    lanes = 128
    with jax.named_scope("walsh1"):
        for j in range(local // lanes):
            tile = pl.ds(j * lanes, lanes)
            turned = walsh([hr[d, :, tile].astype(F32) for d in range(n)])
            for d in range(n):
                bs[d, :, tile] = (turned[d] * factor).astype(BF)
    with jax.named_scope("exch1"):
        for shift in range(1, n):
            to = lax.rem(me + shift, n)
            send(bs.at[to], br.at[c, k], b_send, b_recv.at[c], to)
        pltpu.make_async_copy(bs.at[me], br.at[c, k], b_recv.at[c]).start()

    limit = 127.0 * clip[...]

    def clipped(h):
        with jax.named_scope(f"cwait{h}"):
            settle(br.at[h], b_recv.at[h])
        for q in range(chips // 2):
            values = jnp.concatenate([br[h, 2 * q].astype(F32), br[h, 2 * q + 1].astype(F32)], axis=0)
            y[h, pl.ds(2 * q * rows, 2 * rows), :] = jnp.clip(values, -limit, limit).astype(BF)

    def down(h, t):
        part = pl.ds(pl.multiple_of(t * ospan, ospan), ospan)
        if h == 0:
            pltpu.make_async_copy(wd.at[:, part], vd.at[:, part], dsem.at[t]).wait()
        own[h, t] = jnp.dot(y[h], vd[:, part], preferred_element_type=F32).reshape(chips, rows, ospan)

        @pl.when(c != h)
        def _():
            cs[t] = own[h, t].astype(BF)
            send(cs.at[t], cr.at[t], rs_send.at[0], rc_recv.at[t], core_peer)

    def over_rows(t):
        settle(cr.at[t], rc_recv.at[t])
        for nth in range(line):
            at = lax.rem(a + nth, line) * 2 + 1 - b
            ys[t, nth] = (own[c, t, at] + cr[t, at].astype(F32)).astype(BF)
        far = pl.ds(1, line - 1)
        send(ys.at[t, far], yr.at[t, far], rs_send.at[1], ry_recv.at[t, 1], y_peer)

    def own_rows():
        for t in range(OUT_STEPS):
            send(ys.at[t, 0], yr.at[t, 0], rs_send.at[1], ry_recv.at[t, 0], y_peer)

    def column(t, at):
        landed = yr[t, lax.rem(at - a + line, line)].astype(F32)
        return own[c, t, at * 2 + b] + cr[t, at * 2 + b].astype(F32) + landed

    def to_mate(t):
        settle(yr.at[t, pl.ds(1, line - 1)], ry_recv.at[t, 1])
        for at in range(line):
            @pl.when(outward(at))
            def _():
                zs[t, at] = column(t, at).astype(BF)
                send(zs.at[t, at], zr.at[t, at], rs_send.at[2], rz_recv.at[t, at], device(mate))

    def to_line(t):
        for at in range(line):
            @pl.when(inward(at))
            def _():
                settle(zr.at[t, at], rz_recv.at[t, at])
                zs[t, at] = (column(t, at) + zr[t, at].astype(F32)).astype(BF)
                send(zs.at[t, at], pr.at[t, a // 2], rs_send.at[2], rp_recv.at[t, a // 2], device(at))

    def finish(t):
        settle(yr.at[t, 0], ry_recv.at[t, 0])
        settle(zr.at[t, a], rz_recv.at[t, a])
        values = column(t, a) + zr[t, a].astype(F32)
        for step in range(1, line // 2):
            pair = lax.rem(a // 2 + step, line // 2)
            settle(pr.at[t, pair], rp_recv.at[t, pair])
            values = values + pr[t, pair].astype(F32)
        part = pl.ds(pl.multiple_of(t * ospan, ospan), ospan)
        out[:, part] = (tok[:, part].astype(F32) + values).astype(out.dtype)

    def stages(u):
        @pl.when(u == LATE)
        def _():
            own_rows()

        for (first, last), stage in zip(LAG, (over_rows, to_mate, to_line, finish)):
            t = u - first - (last - first) * c

            @pl.when((t >= 0) & (t < OUT_STEPS))
            def _():
                with jax.named_scope(stage.__name__):
                    stage(t)

    def run(h, start, count):
        @pl.loop(0, count)
        def _(i):
            if h is not None:
                with jax.named_scope("down"):
                    down(h, i)
            stages(start + i)

    clipped(0)
    run(0, 0, OUT_STEPS)
    clipped(1)
    run(1, OUT_STEPS, OUT_STEPS)
    run(None, 2 * OUT_STEPS, LAG[-1][1] - OUT_STEPS)

    with jax.named_scope("drain"):
        for copies in range(1, line):
            @pl.when(jnp.where(odd == 0, a, line - 1 - a) == copies)
            def _():
                settle(x.at[0, pl.ds(0, copies)], relay_send)
        settle(x.at[0], core_send)
        settle(x.at[0, pl.ds(0, line + line // 2)], ag_send)
        settle(hr.at[pl.ds(0, n - 1)], a_send)
        settle(hr.at[pl.ds(0, n - 1)], b_send)
        settle(cs, rs_send.at[0])
        settle(ys, rs_send.at[1])
        settle(zs.at[:, pl.ds(0, line - 1)], rs_send.at[2])


def layer(n, tokens, norm_gain, gate_weight, up_weight, down_weight, clip_scale):
    rows, width = tokens.shape
    local = gate_weight.shape[1]
    outs = down_weight.shape[1]
    line, chips = n // 4, n // 2
    total = n * rows
    ospan = outs // OUT_STEPS
    vmem = pl.BlockSpec(memory_space=pltpu.VMEM)
    hbm = pl.BlockSpec(memory_space=pl.ANY)
    dma = pltpu.SemaphoreType.DMA
    return pl.pallas_call(
        functools.partial(kernel, n),
        out_shape=jax.ShapeDtypeStruct((rows, outs), BF),
        in_specs=[vmem, vmem, hbm, hbm, hbm, vmem],
        out_specs=vmem,
        scratch_shapes=[
            pltpu.VMEM((2, chips, rows, width), BF),
            pltpu.VMEM((width, local), BF),
            pltpu.VMEM((width, local), BF),
            pltpu.VMEM((local, outs), BF),
            pltpu.VMEM((total, local), F32),
            pltpu.VMEM((total, local), F32),
            pltpu.VMEM((BLOCK, BLOCK), BF),
            pltpu.VMEM((2, chips, rows, local), BF),
            pltpu.VMEM((n, rows, local), BF),
            pltpu.VMEM((n, rows, local), BF),
            pltpu.VMEM((2, chips, rows, local), BF),
            pltpu.VMEM((2, chips * rows, local), BF),
            pltpu.VMEM((2, OUT_STEPS, chips, rows, ospan), F32),
            pltpu.VMEM((OUT_STEPS, chips, rows, ospan), BF),
            pltpu.VMEM((OUT_STEPS, chips, rows, ospan), BF),
            pltpu.VMEM((OUT_STEPS, line, rows, ospan), BF),
            pltpu.VMEM((OUT_STEPS, line, rows, ospan), BF),
            pltpu.VMEM((OUT_STEPS, line, rows, ospan), BF),
            pltpu.VMEM((OUT_STEPS, line, rows, ospan), BF),
            pltpu.VMEM((OUT_STEPS, line // 2, rows, ospan), BF),
            dma((2, STEPS)), dma((OUT_STEPS,)), dma(()), dma(()), dma(()),
            dma((STEPS, line)), dma((STEPS, line)), dma((STEPS,)),
            dma(()), dma(()), dma(()), dma((2,)), dma((3,)),
            dma((OUT_STEPS,)), dma((OUT_STEPS, 2)), dma((OUT_STEPS, line)), dma((OUT_STEPS, line // 2)),
        ],
        compiler_params=pltpu.CompilerParams(
            collective_id=0, has_side_effects=True, vmem_limit_bytes=67043328),
    )(tokens, norm_gain.reshape(1, -1), gate_weight, up_weight, down_weight, clip_scale.reshape(1, -1))


def solution(mesh):
    in_specs = (
        P(("groups", "hid"), None),
        P(),
        P(None, "hid"),
        P(None, "hid"),
        P("hid", None),
        P("hid"),
    )
    return jax.shard_map(
        functools.partial(layer, mesh.shape["hid"]), mesh=mesh, in_specs=in_specs,
        out_specs=P(("groups", "hid"), None), check_vma=False)
```

```python
import functools
import math

import jax
import jax.numpy as jnp
from jax import lax
from jax.experimental import pallas as pl
from jax.experimental.pallas import tpu as pltpu
from jax.sharding import PartitionSpec as P

BLOCK = 256
STEPS = 8
OUT_STEPS = 8
AHEAD = 8
HEAD = 4
LAG = ((2, 6), (8, 14), (10, 16), (18, 24))
LATE = (17, 14)
MESH = pl.DeviceIdType.MESH
BF = jnp.bfloat16
F32 = jnp.float32


def walsh(parts):
    parts = list(parts)
    half = 1
    while half < len(parts):
        for at in range(len(parts)):
            if at & half == 0:
                low, high = parts[at], parts[at + half]
                parts[at], parts[at + half] = low + high, low - high
        half *= 2
    return parts


def kernel(n, tok_in, gain_in, wg, wu, wd, clip_in, out,
           tok, gain, clip, x, vg, vu, vd, gate, up, table, hs, hr, bs, br, y,
           own, cs, cr, ys, yr, zs, zr, pr,
           in_sem, wsem, dsem, ag_send, core_send, relay_send, z_recv, y_recv, c_recv,
           a_send, b_send, a_recv, b_recv, rs_send,
           rc_recv, ry_recv, rz_recv, rp_recv):
    me = lax.axis_index("hid")
    line, chips = n // 4, n // 2
    a, b, c = me // 4, (me // 2) % 2, me % 2
    k = me // 2
    odd = a % 2
    mate = a + 1 - 2 * odd
    rows, width = tok.shape
    local = vg.shape[1]
    span = width // STEPS
    ospan = out.shape[1] // OUT_STEPS
    core_peer = me + 1 - 2 * c
    y_peer = (a * 2 + 1 - b) * 2 + c

    def device(a_at):
        return (a_at * 2 + b) * 2 + c

    def other(nth):
        down = jnp.where(a == 0, 1 + nth, lax.rem(a + line - 1 - nth, line))
        up = jnp.where(a == line - 1, line - 2 - nth, lax.rem(a + 1 + nth, line))
        return jnp.where(odd == 0, down, up)

    def outward(a_at):
        return jnp.where(odd == 0, a_at > a, a_at < a)

    def inward(a_at):
        return jnp.where(odd == 0, a_at < a, a_at > a)

    def send(src, dst, ssem, rsem, to):
        pltpu.make_async_remote_copy(
            src_ref=src, dst_ref=dst, send_sem=ssem, recv_sem=rsem,
            device_id={"hid": to}, device_id_type=MESH).start()

    def settle(ref, sem):
        pltpu.make_async_copy(ref, ref, sem).wait()

    barrier = pltpu.get_barrier_semaphore()

    def greet(to):
        pl.semaphore_signal(barrier, inc=1, device_id={"hid": to}, device_id_type=MESH)

    greet(core_peer)
    greet(y_peer)
    greet(device(mate))
    for at in range(line):
        @pl.when(inward(at))
        def _():
            greet(device(at))

    inputs = [pltpu.make_async_copy(src, dst, in_sem.at[at])
              for at, (src, dst) in enumerate(((tok_in, tok), (gain_in, gain), (clip_in, clip)))]
    for copy in inputs:
        copy.start()

    at_row = lax.broadcasted_iota(jnp.int32, (BLOCK, BLOCK), 0)
    at_col = lax.broadcasted_iota(jnp.int32, (BLOCK, BLOCK), 1)
    bits = at_row & at_col
    folded = bits
    for place in range(1, (BLOCK - 1).bit_length()):
        folded = folded ^ (bits >> place)
    table[...] = (1 - 2 * (folded & 1)).astype(F32).astype(BF)

    for copy in inputs:
        copy.wait()

    weight_copies = []
    for s in range(STEPS):
        part = pl.ds(s * span, span)
        weight_copies.append((
            pltpu.make_async_copy(wg.at[part, :], vg.at[part, :], wsem.at[0, s]),
            pltpu.make_async_copy(wu.at[part, :], vu.at[part, :], wsem.at[1, s])))
        for copy in weight_copies[-1]:
            copy.start()
    down_copies = []
    for t in range(OUT_STEPS):
        part = pl.ds(t * ospan, ospan)
        down_copies.append(pltpu.make_async_copy(wd.at[:, part], vd.at[:, part], dsem.at[t]))
        down_copies[-1].start()

    values = tok[...].astype(F32)
    inverse = lax.rsqrt(jnp.mean(values * values, axis=-1, keepdims=True) + 1e-05)
    x[c, k] = (values * inverse * gain[...]).astype(BF)

    with jax.named_scope("barrier"):
        pl.semaphore_wait(barrier, 2 + line // 2)

    def block(a_at, b_at, s):
        return x.at[c, a_at * 2 + b_at, :, pl.ds(s * span, span)]

    def begin_line(s):
        mine = block(a, b, s)
        for step in range(1, line // 2):
            pair = lax.rem(a // 2 + step, line // 2)
            near = 2 * pair + (pair < a // 2).astype(jnp.int32)
            send(mine, mine, ag_send, z_recv.at[s, a], device(near))
        send(mine, mine, ag_send, z_recv.at[s, a], device(mate))

    def begin_rows(s):
        mine = block(a, b, s)
        send(mine, mine, ag_send, y_recv.at[s, a], y_peer)
        send(mine, mine, core_send, c_recv.at[s], core_peer)

    for s in range(STEPS):
        if s < AHEAD:
            begin_line(s)
        begin_rows(s)

    def relay_line(s, first, last):
        for nth in range(first, last):
            src = other(nth)
            got = block(src, b, s)
            settle(got, z_recv.at[s, src])

            @pl.when(inward(src))
            def _():
                send(got, got, relay_send, z_recv.at[s, src], device(mate))
            send(got, got, ag_send, y_recv.at[s, src], y_peer)
            send(got, got, core_send, c_recv.at[s], core_peer)

    def relay_rows(s):
        for nth in range(line):
            src = a if nth == 0 else other(nth - 1)
            got = block(src, 1 - b, s)
            settle(got, y_recv.at[s, src])
            send(got, got, core_send, c_recv.at[s], core_peer)

    def project(s):
        part = pl.ds(s * span, span)
        with jax.named_scope("pwait"):
            settle(x.at[1 - c, :, :, part], c_recv.at[s])
        with jax.named_scope("wwait"):
            for copy in weight_copies[s]:
                copy.wait()
        left = x[:, :, :, part].reshape(n * rows, span)
        for acc, weight in ((gate, vg), (up, vu)):
            term = jnp.dot(left, weight[part, :], preferred_element_type=F32)
            acc[...] = term if s == 0 else acc[...] + term

    outer = (a == 0) | (a == line - 1)

    @pl.when(outer)
    def _():
        for s in range(STEPS):
            with jax.named_scope(f"relay_first{s}"):
                relay_line(s, 0, 1)

    for s in range(STEPS + 5):
        if s < STEPS:
            with jax.named_scope(f"relay_line{s}"):
                @pl.when(jnp.logical_not(outer))
                def _():
                    relay_line(s, 0, 1)
                relay_line(s, 1, line - 1)
        if 0 <= s - 4 < STEPS:
            with jax.named_scope(f"relay_rows{s-4}"):
                relay_rows(s - 4)
        if 0 <= s - 5 < STEPS:
            with jax.named_scope(f"project{s-5}"):
                project(s - 5)

    half = chips * rows
    for h in range(2):
        with jax.named_scope(f"swiglu{h}"):
            group = pl.ds(h * half, half)
            for at in range(local // BLOCK):
                tile = pl.ds(at * BLOCK, BLOCK)
                value = gate[group, tile]
                hidden = value / (1.0 + jnp.exp(-value)) * up[group, tile]
                gate[group, tile] = jnp.dot(hidden.astype(BF), table[...], preferred_element_type=F32)
            for q in range(chips):
                values = gate[pl.ds((h * chips + q) * rows, rows), :]
                turned = walsh([values[:, at * BLOCK:(at + 1) * BLOCK] for at in range(local // BLOCK)])
                hs[h, q] = (turned[0] if len(turned) == 1 else jnp.concatenate(turned, axis=1)).astype(BF)
            for shift in range(1, chips):
                q = lax.rem(k + shift, chips)
                send(hs.at[h, q], hr.at[me], a_send, a_recv, q * 2 + h)

            @pl.when(c == h)
            def _():
                pltpu.make_async_copy(hs.at[h, k], hr.at[me], a_recv).start()

            @pl.when(c != h)
            def _():
                send(hs.at[h, k], hr.at[me], a_send, a_recv, core_peer)

    with jax.named_scope("exch0"):
        settle(hr, a_recv)
    factor = 1.0 / math.sqrt(n * local)
    lanes = 128
    with jax.named_scope("walsh1"):
        for j in range(local // lanes):
            tile = pl.ds(j * lanes, lanes)
            turned = walsh([hr[d, :, tile].astype(F32) for d in range(n)])
            for d in range(n):
                bs[d, :, tile] = (turned[d] * factor).astype(BF)
    with jax.named_scope("exch1"):
        for shift in range(1, n):
            to = lax.rem(me + shift, n)
            send(bs.at[to], br.at[c, k], b_send, b_recv.at[c], to)
        pltpu.make_async_copy(bs.at[me], br.at[c, k], b_recv.at[c]).start()

    limit = 127.0 * clip[...]

    def clipped(h):
        with jax.named_scope(f"cwait{h}"):
            settle(br.at[h], b_recv.at[h])
        for q in range(chips // 2):
            values = jnp.concatenate([br[h, 2 * q].astype(F32), br[h, 2 * q + 1].astype(F32)], axis=0)
            y[h, pl.ds(2 * q * rows, 2 * rows), :] = jnp.clip(values, -limit, limit).astype(BF)

    def down(hs_, t):
        part = pl.ds(pl.multiple_of(t * ospan, ospan), ospan)
        if 0 in hs_:
            pltpu.make_async_copy(wd.at[:, part], vd.at[:, part], dsem.at[t]).wait()
        left = y[hs_[0]] if len(hs_) == 1 else y[...].reshape(2 * half, local)
        result = jnp.dot(left, vd[:, part], preferred_element_type=F32)
        if len(hs_) == 1:
            own[hs_[0], t] = result.reshape(chips, rows, ospan)
        else:
            own[:, t] = result.reshape(2, chips, rows, ospan)

        def share():
            cs[t] = own[1 - c, t].astype(BF)
            send(cs.at[t], cr.at[t], rs_send.at[0], rc_recv.at[t], core_peer)

        if len(hs_) == 1:
            pl.when(c != hs_[0])(share)
        else:
            share()

    def over_rows(t):
        settle(cr.at[t], rc_recv.at[t])
        for nth in range(line):
            at = lax.rem(a + nth, line) * 2 + 1 - b
            ys[t, nth] = (own[c, t, at] + cr[t, at].astype(F32)).astype(BF)
        far = pl.ds(1, line - 1)
        send(ys.at[t, far], yr.at[t, far], rs_send.at[1], ry_recv.at[t, 1], y_peer)

    def own_rows():
        for t in range(OUT_STEPS):
            send(ys.at[t, 0], yr.at[t, 0], rs_send.at[1], ry_recv.at[t, 0], y_peer)

    def column(t, at):
        landed = yr[t, lax.rem(at - a + line, line)].astype(F32)
        return own[c, t, at * 2 + b] + cr[t, at * 2 + b].astype(F32) + landed

    def to_mate(t):
        settle(yr.at[t, pl.ds(1, line - 1)], ry_recv.at[t, 1])
        for at in range(line):
            @pl.when(outward(at))
            def _():
                zs[t, at] = column(t, at).astype(BF)
                send(zs.at[t, at], zr.at[t, at], rs_send.at[2], rz_recv.at[t, at], device(mate))

    def to_line(t):
        for at in range(line):
            @pl.when(inward(at))
            def _():
                settle(zr.at[t, at], rz_recv.at[t, at])
                zs[t, at] = (column(t, at) + zr[t, at].astype(F32)).astype(BF)
                send(zs.at[t, at], pr.at[t, a // 2], rs_send.at[2], rp_recv.at[t, a // 2], device(at))

    def finish(t):
        settle(yr.at[t, 0], ry_recv.at[t, 0])
        settle(zr.at[t, a], rz_recv.at[t, a])
        values = column(t, a) + zr[t, a].astype(F32)
        for step in range(1, line // 2):
            pair = lax.rem(a // 2 + step, line // 2)
            settle(pr.at[t, pair], rp_recv.at[t, pair])
            values = values + pr[t, pair].astype(F32)
        part = pl.ds(pl.multiple_of(t * ospan, ospan), ospan)
        out[:, part] = (tok[:, part].astype(F32) + values).astype(out.dtype)

    def stages(u):
        @pl.when(u == LATE[0] + (LATE[1] - LATE[0]) * c)
        def _():
            own_rows()

        for (first, last), stage in zip(LAG, (over_rows, to_mate, to_line, finish)):
            t = u - first - (last - first) * c

            @pl.when((t >= 0) & (t < OUT_STEPS))
            def _():
                with jax.named_scope(stage.__name__):
                    stage(lax.rem(t + HEAD * c, OUT_STEPS))

    def run(hs_, start, count, base=0):
        @pl.loop(0, count)
        def _(i):
            if hs_:
                with jax.named_scope("down"):
                    down(hs_, base + i)
            stages(start + i)

    clipped(0)
    run((0,), 0, HEAD)
    clipped(1)
    run((0, 1), HEAD, OUT_STEPS - HEAD, HEAD)
    run((1,), OUT_STEPS, HEAD)
    run((), OUT_STEPS + HEAD, LAG[-1][1] - HEAD)

    with jax.named_scope("drain"):
        for copies in range(1, line):
            @pl.when(jnp.where(odd == 0, a, line - 1 - a) == copies)
            def _():
                settle(x.at[0, pl.ds(0, copies)], relay_send)
        settle(x.at[0], core_send)
        settle(x.at[0, pl.ds(0, line + line // 2)], ag_send)
        settle(hr.at[pl.ds(0, n - 1)], a_send)
        settle(hr.at[pl.ds(0, n - 1)], b_send)
        settle(cs, rs_send.at[0])
        settle(ys, rs_send.at[1])
        settle(zs.at[:, pl.ds(0, line - 1)], rs_send.at[2])


def layer(n, tokens, norm_gain, gate_weight, up_weight, down_weight, clip_scale):
    rows, width = tokens.shape
    local = gate_weight.shape[1]
    outs = down_weight.shape[1]
    line, chips = n // 4, n // 2
    total = n * rows
    ospan = outs // OUT_STEPS
    vmem = pl.BlockSpec(memory_space=pltpu.VMEM)
    hbm = pl.BlockSpec(memory_space=pl.ANY)
    dma = pltpu.SemaphoreType.DMA
    return pl.pallas_call(
        functools.partial(kernel, n),
        out_shape=pltpu.VMEM((rows, outs), BF),
        in_specs=[hbm, hbm, hbm, hbm, hbm, hbm],
        out_specs=vmem,
        scratch_shapes=[
            pltpu.VMEM((rows, width), BF),
            pltpu.VMEM((1, width), F32),
            pltpu.VMEM((1, local), F32),
            pltpu.VMEM((2, chips, rows, width), BF),
            pltpu.VMEM((width, local), BF),
            pltpu.VMEM((width, local), BF),
            pltpu.VMEM((local, outs), BF),
            pltpu.VMEM((total, local), F32),
            pltpu.VMEM((total, local), F32),
            pltpu.VMEM((BLOCK, BLOCK), BF),
            pltpu.VMEM((2, chips, rows, local), BF),
            pltpu.VMEM((n, rows, local), BF),
            pltpu.VMEM((n, rows, local), BF),
            pltpu.VMEM((2, chips, rows, local), BF),
            pltpu.VMEM((2, chips * rows, local), BF),
            pltpu.VMEM((2, OUT_STEPS, chips, rows, ospan), F32),
            pltpu.VMEM((OUT_STEPS, chips, rows, ospan), BF),
            pltpu.VMEM((OUT_STEPS, chips, rows, ospan), BF),
            pltpu.VMEM((OUT_STEPS, line, rows, ospan), BF),
            pltpu.VMEM((OUT_STEPS, line, rows, ospan), BF),
            pltpu.VMEM((OUT_STEPS, line, rows, ospan), BF),
            pltpu.VMEM((OUT_STEPS, line, rows, ospan), BF),
            pltpu.VMEM((OUT_STEPS, line // 2, rows, ospan), BF),
            dma((3,)), dma((2, STEPS)), dma((OUT_STEPS,)), dma(()), dma(()), dma(()),
            dma((STEPS, line)), dma((STEPS, line)), dma((STEPS,)),
            dma(()), dma(()), dma(()), dma((2,)), dma((3,)),
            dma((OUT_STEPS,)), dma((OUT_STEPS, 2)), dma((OUT_STEPS, line)), dma((OUT_STEPS, line // 2)),
        ],
        compiler_params=pltpu.CompilerParams(
            collective_id=0, has_side_effects=True, vmem_limit_bytes=65000000),
    )(tokens, norm_gain.reshape(1, -1), gate_weight, up_weight, down_weight, clip_scale.reshape(1, -1))


def solution(mesh):
    in_specs = (
        P(("groups", "hid"), None),
        P(),
        P(None, "hid"),
        P(None, "hid"),
        P("hid", None),
        P("hid"),
    )
    return jax.shard_map(
        functools.partial(layer, mesh.shape["hid"]), mesh=mesh, in_specs=in_specs,
        out_specs=P(("groups", "hid"), None), check_vma=False)
```

```python
import functools
import math

import jax
import jax.numpy as jnp
from jax import lax
from jax.experimental import pallas as pl
from jax.experimental.pallas import tpu as pltpu
from jax.sharding import PartitionSpec as P

BLOCK = 256
STEPS = 8
OUT_STEPS = 8
AHEAD = 8
BEHIND = 4
HEAD = 4
TURNED = 1
LAG = ((2, 6), (8, 14), (10, 16), (18, 24))
TURNED_LAG = ((2, 6), (7, 11), (13, 17), (18, 24))
LATE = (17, 14)
MESH = pl.DeviceIdType.MESH
BF = jnp.bfloat16
F32 = jnp.float32


def walsh(parts):
    parts = list(parts)
    half = 1
    while half < len(parts):
        for at in range(len(parts)):
            if at & half == 0:
                low, high = parts[at], parts[at + half]
                parts[at], parts[at + half] = low + high, low - high
        half *= 2
    return parts


def kernel(n, tok_in, gain_in, wg, wu, wd, clip_in, out,
           tok, gain, clip, x, vg, vu, vd, gate, up, table, hs, hr, bs, br, y,
           own, cs, cr, ys, yr, zs, zr, pr, zs2, zr2, pr2, yo, yi,
           in_sem, wsem, dsem, ag_send, core_send, relay_send, z_recv, y_recv, c_recv,
           a_send, b_send, a_recv, b_recv, rs_send,
           rc_recv, ry_recv, rz_recv, rp_recv, sz_recv, sp_recv, sy_recv):
    me = lax.axis_index("hid")
    line, chips = n // 4, n // 2
    a, b, c = me // 4, (me // 2) % 2, me % 2
    k = me // 2
    odd = a % 2
    mate = a + 1 - 2 * odd
    rows, width = tok.shape
    local = vg.shape[1]
    span = width // STEPS
    ospan = out.shape[1] // OUT_STEPS
    core_peer = me + 1 - 2 * c
    y_peer = (a * 2 + 1 - b) * 2 + c

    def device(a_at):
        return (a_at * 2 + b) * 2 + c

    def other(nth):
        down = jnp.where(a == 0, 1 + nth, lax.rem(a + line - 1 - nth, line))
        up = jnp.where(a == line - 1, line - 2 - nth, lax.rem(a + 1 + nth, line))
        return jnp.where(odd == 0, down, up)

    def outward(a_at):
        return jnp.where(odd == 0, a_at > a, a_at < a)

    def inward(a_at):
        return jnp.where(odd == 0, a_at < a, a_at > a)

    def send(src, dst, ssem, rsem, to):
        pltpu.make_async_remote_copy(
            src_ref=src, dst_ref=dst, send_sem=ssem, recv_sem=rsem,
            device_id={"hid": to}, device_id_type=MESH).start()

    def settle(ref, sem):
        pltpu.make_async_copy(ref, ref, sem).wait()

    barrier = pltpu.get_barrier_semaphore()

    def greet(to):
        pl.semaphore_signal(barrier, inc=1, device_id={"hid": to}, device_id_type=MESH)

    greet(core_peer)
    greet(y_peer)
    greet(device(mate))
    for at in range(line):
        @pl.when(inward(at))
        def _():
            greet(device(at))

    inputs = [pltpu.make_async_copy(src, dst, in_sem.at[at])
              for at, (src, dst) in enumerate(((tok_in, tok), (gain_in, gain), (clip_in, clip)))]
    for copy in inputs:
        copy.start()

    at_row = lax.broadcasted_iota(jnp.int32, (BLOCK, BLOCK), 0)
    at_col = lax.broadcasted_iota(jnp.int32, (BLOCK, BLOCK), 1)
    bits = at_row & at_col
    folded = bits
    for place in range(1, (BLOCK - 1).bit_length()):
        folded = folded ^ (bits >> place)
    table[...] = (1 - 2 * (folded & 1)).astype(F32).astype(BF)

    for copy in inputs:
        copy.wait()

    weight_copies = []
    for s in range(STEPS):
        part = pl.ds(s * span, span)
        weight_copies.append((
            pltpu.make_async_copy(wg.at[part, :], vg.at[part, :], wsem.at[0, s]),
            pltpu.make_async_copy(wu.at[part, :], vu.at[part, :], wsem.at[1, s])))
        for copy in weight_copies[-1]:
            copy.start()
    down_copies = []
    for t in range(OUT_STEPS):
        part = pl.ds(t * ospan, ospan)
        down_copies.append(pltpu.make_async_copy(wd.at[:, part], vd.at[:, part], dsem.at[t]))
        down_copies[-1].start()

    values = tok[...].astype(F32)
    inverse = lax.rsqrt(jnp.mean(values * values, axis=-1, keepdims=True) + 1e-05)
    x[c, k] = (values * inverse * gain[...]).astype(BF)

    with jax.named_scope("barrier"):
        pl.semaphore_wait(barrier, 2 + line // 2)

    def block(a_at, b_at, s):
        return x.at[c, a_at * 2 + b_at, :, pl.ds(s * span, span)]

    def begin_line(s):
        mine = block(a, b, s)
        for step in range(1, line // 2):
            pair = lax.rem(a // 2 + step, line // 2)
            near = 2 * pair + (pair < a // 2).astype(jnp.int32)
            send(mine, mine, ag_send, z_recv.at[s, a], device(near))
        send(mine, mine, ag_send, z_recv.at[s, a], device(mate))

    def begin_rows(s):
        mine = block(a, b, s)
        send(mine, mine, ag_send, y_recv.at[s, a], y_peer)
        send(mine, mine, core_send, c_recv.at[s], core_peer)

    for s in range(STEPS):
        if s < AHEAD:
            begin_line(s)
        begin_rows(s)

    def relay_line(s, first, last):
        for nth in range(first, last):
            src = other(nth)
            got = block(src, b, s)
            settle(got, z_recv.at[s, src])

            @pl.when(inward(src))
            def _():
                send(got, got, relay_send, z_recv.at[s, src], device(mate))
            send(got, got, ag_send, y_recv.at[s, src], y_peer)
            send(got, got, core_send, c_recv.at[s], core_peer)

    def relay_rows(s):
        for nth in range(line):
            src = a if nth == 0 else other(nth - 1)
            got = block(src, 1 - b, s)
            settle(got, y_recv.at[s, src])
            send(got, got, core_send, c_recv.at[s], core_peer)

    def project(s):
        part = pl.ds(s * span, span)
        with jax.named_scope("pwait"):
            settle(x.at[1 - c, :, :, part], c_recv.at[s])
        with jax.named_scope("wwait"):
            for copy in weight_copies[s]:
                copy.wait()
        left = x[:, :, :, part].reshape(n * rows, span)
        for acc, weight in ((gate, vg), (up, vu)):
            term = jnp.dot(left, weight[part, :], preferred_element_type=F32)
            acc[...] = term if s == 0 else acc[...] + term

    outer = (a == 0) | (a == line - 1)

    @pl.when(outer)
    def _():
        for s in range(STEPS):
            with jax.named_scope(f"relay_first{s}"):
                relay_line(s, 0, 1)

    inner = jnp.logical_not(outer)
    for s in range(STEPS + BEHIND + 1):
        if s < STEPS:
            with jax.named_scope(f"relay_line{s}"):
                if s <= BEHIND:
                    @pl.when(inner)
                    def _():
                        relay_line(s, 0, 1)
                    relay_line(s, 1, line - 1)
                else:
                    @pl.when(outer)
                    def _():
                        relay_line(s, 1, line - 1)
        if s == BEHIND:
            @pl.when(inner)
            def _():
                for later in range(BEHIND + 1, STEPS):
                    relay_line(later, 0, line - 1)
        if 0 <= s - BEHIND < STEPS:
            with jax.named_scope(f"relay_rows{s-BEHIND}"):
                relay_rows(s - BEHIND)
        if 0 <= s - BEHIND - 1 < STEPS:
            with jax.named_scope(f"project{s-BEHIND-1}"):
                project(s - BEHIND - 1)

    half = chips * rows
    for h in range(2):
        with jax.named_scope(f"swiglu{h}"):
            group = pl.ds(h * half, half)
            for at in range(local // BLOCK):
                tile = pl.ds(at * BLOCK, BLOCK)
                value = gate[group, tile]
                hidden = value / (1.0 + jnp.exp(-value)) * up[group, tile]
                gate[group, tile] = jnp.dot(hidden.astype(BF), table[...], preferred_element_type=F32)
            for q in range(chips):
                values = gate[pl.ds((h * chips + q) * rows, rows), :]
                turned = walsh([values[:, at * BLOCK:(at + 1) * BLOCK] for at in range(local // BLOCK)])
                hs[h, q] = (turned[0] if len(turned) == 1 else jnp.concatenate(turned, axis=1)).astype(BF)
            for shift in range(1, chips):
                q = lax.rem(k + shift, chips)
                send(hs.at[h, q], hr.at[me], a_send, a_recv, q * 2 + h)

            @pl.when(c == h)
            def _():
                pltpu.make_async_copy(hs.at[h, k], hr.at[me], a_recv).start()

            @pl.when(c != h)
            def _():
                send(hs.at[h, k], hr.at[me], a_send, a_recv, core_peer)

    with jax.named_scope("exch0"):
        settle(hr, a_recv)
    factor = 1.0 / math.sqrt(n * local)
    lanes = 128
    with jax.named_scope("walsh1"):
        for j in range(local // lanes):
            tile = pl.ds(j * lanes, lanes)
            turned = walsh([hr[d, :, tile].astype(F32) for d in range(n)])
            for d in range(n):
                bs[d, :, tile] = (turned[d] * factor).astype(BF)
    with jax.named_scope("exch1"):
        for shift in range(1, n):
            to = lax.rem(me + shift, n)
            send(bs.at[to], br.at[c, k], b_send, b_recv.at[c], to)
        pltpu.make_async_copy(bs.at[me], br.at[c, k], b_recv.at[c]).start()

    limit = 127.0 * clip[...]

    def clipped(h):
        with jax.named_scope(f"cwait{h}"):
            settle(br.at[h], b_recv.at[h])
        for q in range(chips // 2):
            values = jnp.concatenate([br[h, 2 * q].astype(F32), br[h, 2 * q + 1].astype(F32)], axis=0)
            y[h, pl.ds(2 * q * rows, 2 * rows), :] = jnp.clip(values, -limit, limit).astype(BF)

    def down(hs_, t):
        part = pl.ds(pl.multiple_of(t * ospan, ospan), ospan)
        if 0 in hs_:
            pltpu.make_async_copy(wd.at[:, part], vd.at[:, part], dsem.at[t]).wait()
        left = y[hs_[0]] if len(hs_) == 1 else y[...].reshape(2 * half, local)
        result = jnp.dot(left, vd[:, part], preferred_element_type=F32)
        if len(hs_) == 1:
            own[hs_[0], t] = result.reshape(chips, rows, ospan)
        else:
            own[:, t] = result.reshape(2, chips, rows, ospan)

        def share():
            cs[t] = own[1 - c, t].astype(BF)
            send(cs.at[t], cr.at[t], rs_send.at[0], rc_recv.at[t], core_peer)

        if len(hs_) == 1:
            pl.when(c != hs_[0])(share)
        else:
            share()

    def order(at):
        return lax.rem(at + HEAD * c, OUT_STEPS)

    def over_rows(nth_step):
        t = order(nth_step)
        settle(cr.at[t], rc_recv.at[t])
        for nth in range(line):
            at = lax.rem(a + nth, line) * 2 + 1 - b
            ys[t, nth] = (own[c, t, at] + cr[t, at].astype(F32)).astype(BF)
        far = pl.ds(1, line - 1)
        send(ys.at[t, far], yr.at[t, far], rs_send.at[1], ry_recv.at[t, 1], y_peer)

    def own_rows():
        for at in range(TURNED, OUT_STEPS):
            t = order(at)
            send(ys.at[t, 0], yr.at[t, 0], rs_send.at[1], ry_recv.at[t, 0], y_peer)

    def column(t, at):
        landed = yr[t, lax.rem(at - a + line, line)].astype(F32)
        return own[c, t, at * 2 + b] + cr[t, at * 2 + b].astype(F32) + landed

    def to_mate(nth_step):
        t = order(nth_step)
        settle(yr.at[t, pl.ds(1, line - 1)], ry_recv.at[t, 1])
        for at in range(line):
            @pl.when(outward(at))
            def _():
                zs[t, at] = column(t, at).astype(BF)
                send(zs.at[t, at], zr.at[t, at], rs_send.at[2], rz_recv.at[t, at], device(mate))

    def to_line(nth_step):
        t = order(nth_step)
        for at in range(line):
            @pl.when(inward(at))
            def _():
                settle(zr.at[t, at], rz_recv.at[t, at])
                zs[t, at] = (column(t, at) + zr[t, at].astype(F32)).astype(BF)
                send(zs.at[t, at], pr.at[t, a // 2], rs_send.at[2], rp_recv.at[t, a // 2], device(at))

    def finish(nth_step):
        t = order(nth_step)
        settle(yr.at[t, 0], ry_recv.at[t, 0])
        settle(zr.at[t, a], rz_recv.at[t, a])
        values = column(t, a) + zr[t, a].astype(F32)
        for step in range(1, line // 2):
            pair = lax.rem(a // 2 + step, line // 2)
            settle(pr.at[t, pair], rp_recv.at[t, pair])
            values = values + pr[t, pair].astype(F32)
        part = pl.ds(pl.multiple_of(t * ospan, ospan), ospan)
        out[:, part] = (tok[:, part].astype(F32) + values).astype(out.dtype)

    def turned_mate(i):
        t = order(i)
        settle(cr.at[t], rc_recv.at[t])
        for at in range(line):
            @pl.when(outward(at))
            def _():
                for b_at in range(2):
                    q = at * 2 + b_at
                    zs2[i, at, b_at] = (own[c, t, q] + cr[t, q].astype(F32)).astype(BF)
                send(zs2.at[i, at], zr2.at[i, at], rs_send.at[3], sz_recv.at[i, at], device(mate))

    def turned_line(i):
        t = order(i)
        for at in range(line):
            @pl.when(inward(at))
            def _():
                settle(zr2.at[i, at], sz_recv.at[i, at])
                for b_at in range(2):
                    q = at * 2 + b_at
                    zs2[i, at, b_at] = (own[c, t, q] + cr[t, q].astype(F32) + zr2[i, at, b_at].astype(F32)).astype(BF)
                send(zs2.at[i, at], pr2.at[i, a // 2], rs_send.at[3], sp_recv.at[i, a // 2], device(at))

    def line_sum(i, b_at):
        t = order(i)
        q = a * 2 + b_at
        values = own[c, t, q] + cr[t, q].astype(F32) + zr2[i, a, b_at].astype(F32)
        for step in range(1, line // 2):
            pair = lax.rem(a // 2 + step, line // 2)
            values = values + pr2[i, pair, b_at].astype(F32)
        return values

    def turned_rows(i):
        settle(zr2.at[i, a], sz_recv.at[i, a])
        for step in range(1, line // 2):
            pair = lax.rem(a // 2 + step, line // 2)
            settle(pr2.at[i, pair], sp_recv.at[i, pair])
        yo[i] = line_sum(i, 1 - b).astype(BF)
        send(yo.at[i], yi.at[i], rs_send.at[4], sy_recv.at[i], y_peer)

    def turned_finish(i):
        settle(yi.at[i], sy_recv.at[i])
        part = pl.ds(pl.multiple_of(order(i) * ospan, ospan), ospan)
        out[:, part] = (tok[:, part].astype(F32) + line_sum(i, b) + yi[i].astype(F32)).astype(out.dtype)

    table_of_stages = (
        [(lag, stage, 0, TURNED) for lag, stage in zip(TURNED_LAG, (turned_mate, turned_line, turned_rows, turned_finish))]
        + [(lag, stage, TURNED, OUT_STEPS) for lag, stage in zip(LAG, (over_rows, to_mate, to_line, finish))])

    def stages(u):
        @pl.when(u == LATE[0] + (LATE[1] - LATE[0]) * c)
        def _():
            own_rows()

        for (first, last), stage, low, high in table_of_stages:
            i = u - first - (last - first) * c

            @pl.when((i >= low) & (i < high))
            def _():
                with jax.named_scope(stage.__name__):
                    stage(i)

    def run(hs_, start, count, base=0):
        @pl.loop(0, count)
        def _(i):
            if hs_:
                with jax.named_scope("down"):
                    down(hs_, base + i)
            stages(start + i)

    clipped(0)
    run((0,), 0, HEAD)
    clipped(1)
    run((0, 1), HEAD, OUT_STEPS - HEAD, HEAD)
    run((1,), OUT_STEPS, HEAD)
    run((), OUT_STEPS + HEAD, LAG[-1][1] - HEAD)

    with jax.named_scope("drain"):
        for copies in range(1, line):
            @pl.when(jnp.where(odd == 0, a, line - 1 - a) == copies)
            def _():
                settle(x.at[0, pl.ds(0, copies)], relay_send)
        settle(x.at[0], core_send)
        settle(x.at[0, pl.ds(0, line + line // 2)], ag_send)
        settle(hr.at[pl.ds(0, n - 1)], a_send)
        settle(hr.at[pl.ds(0, n - 1)], b_send)
        settle(cs, rs_send.at[0])
        settle(ys.at[pl.ds(0, OUT_STEPS - TURNED)], rs_send.at[1])
        settle(zs.at[pl.ds(0, OUT_STEPS - TURNED), pl.ds(0, line - 1)], rs_send.at[2])
        settle(zs2.at[:, pl.ds(0, line - 1)], rs_send.at[3])
        settle(yo, rs_send.at[4])


def layer(n, tokens, norm_gain, gate_weight, up_weight, down_weight, clip_scale):
    rows, width = tokens.shape
    local = gate_weight.shape[1]
    outs = down_weight.shape[1]
    line, chips = n // 4, n // 2
    total = n * rows
    ospan = outs // OUT_STEPS
    vmem = pl.BlockSpec(memory_space=pltpu.VMEM)
    hbm = pl.BlockSpec(memory_space=pl.ANY)
    dma = pltpu.SemaphoreType.DMA
    return pl.pallas_call(
        functools.partial(kernel, n),
        out_shape=pltpu.VMEM((rows, outs), BF),
        in_specs=[hbm, hbm, hbm, hbm, hbm, hbm],
        out_specs=vmem,
        scratch_shapes=[
            pltpu.VMEM((rows, width), BF),
            pltpu.VMEM((1, width), F32),
            pltpu.VMEM((1, local), F32),
            pltpu.VMEM((2, chips, rows, width), BF),
            pltpu.VMEM((width, local), BF),
            pltpu.VMEM((width, local), BF),
            pltpu.VMEM((local, outs), BF),
            pltpu.VMEM((total, local), F32),
            pltpu.VMEM((total, local), F32),
            pltpu.VMEM((BLOCK, BLOCK), BF),
            pltpu.VMEM((2, chips, rows, local), BF),
            pltpu.VMEM((n, rows, local), BF),
            pltpu.VMEM((n, rows, local), BF),
            pltpu.VMEM((2, chips, rows, local), BF),
            pltpu.VMEM((2, chips * rows, local), BF),
            pltpu.VMEM((2, OUT_STEPS, chips, rows, ospan), F32),
            pltpu.VMEM((OUT_STEPS, chips, rows, ospan), BF),
            pltpu.VMEM((OUT_STEPS, chips, rows, ospan), BF),
            pltpu.VMEM((OUT_STEPS, line, rows, ospan), BF),
            pltpu.VMEM((OUT_STEPS, line, rows, ospan), BF),
            pltpu.VMEM((OUT_STEPS, line, rows, ospan), BF),
            pltpu.VMEM((OUT_STEPS, line, rows, ospan), BF),
            pltpu.VMEM((OUT_STEPS, line // 2, rows, ospan), BF),
            pltpu.VMEM((TURNED, line, 2, rows, ospan), BF),
            pltpu.VMEM((TURNED, line, 2, rows, ospan), BF),
            pltpu.VMEM((TURNED, line // 2, 2, rows, ospan), BF),
            pltpu.VMEM((TURNED, rows, ospan), BF),
            pltpu.VMEM((TURNED, rows, ospan), BF),
            dma((3,)), dma((2, STEPS)), dma((OUT_STEPS,)), dma(()), dma(()), dma(()),
            dma((STEPS, line)), dma((STEPS, line)), dma((STEPS,)),
            dma(()), dma(()), dma(()), dma((2,)), dma((5,)),
            dma((OUT_STEPS,)), dma((OUT_STEPS, 2)), dma((OUT_STEPS, line)), dma((OUT_STEPS, line // 2)),
            dma((TURNED, line)), dma((TURNED, line // 2)), dma((TURNED,)),
        ],
        compiler_params=pltpu.CompilerParams(
            collective_id=0, has_side_effects=True, vmem_limit_bytes=66000000),
    )(tokens, norm_gain.reshape(1, -1), gate_weight, up_weight, down_weight, clip_scale.reshape(1, -1))


def solution(mesh):
    in_specs = (
        P(("groups", "hid"), None),
        P(),
        P(None, "hid"),
        P(None, "hid"),
        P("hid", None),
        P("hid"),
    )
    return jax.shard_map(
        functools.partial(layer, mesh.shape["hid"]), mesh=mesh, in_specs=in_specs,
        out_specs=P(("groups", "hid"), None), check_vma=False)
```

```python
import functools
import math

import jax
import jax.numpy as jnp
from jax import lax
from jax.experimental import pallas as pl
from jax.experimental.pallas import tpu as pltpu
from jax.sharding import PartitionSpec as P

BLOCK = 256
STEPS = 8
OUT_STEPS = 8
AHEAD = 8
BEHIND = 4
HEAD = 4
TURNED = 1
LAG = ((2, 6), (8, 14), (10, 16), (18, 24))
TURNED_LAG = ((2, 6), (7, 11), (13, 17), (18, 24))
LATE = (17, 14)
MESH = pl.DeviceIdType.MESH
BF = jnp.bfloat16
F32 = jnp.float32


def walsh(parts):
    parts = list(parts)
    half = 1
    while half < len(parts):
        for at in range(len(parts)):
            if at & half == 0:
                low, high = parts[at], parts[at + half]
                parts[at], parts[at + half] = low + high, low - high
        half *= 2
    return parts


def kernel(n, tok_in, gain_in, wg, wu, wd, clip_in, out,
           tok, gain, clip, x, vg, vu, vd, gate, up, table, hs, hr, bs, br, y,
           own, cs, cr, ys, yr, zs, zr, pr, zs2, zr2, pr2, yo, yi,
           in_sem, wsem, dsem, ag_send, core_send, relay_send, z_recv, y_recv, c_recv,
           a_send, b_send, a_recv, b_recv, rs_send, sz_recv, sp_recv, sy_recv):
    rc_recv, rz_recv = c_recv, z_recv
    me = lax.axis_index("hid")
    line, chips = n // 4, n // 2
    a, b, c = me // 4, (me // 2) % 2, me % 2
    k = me // 2
    odd = a % 2
    mate = a + 1 - 2 * odd
    rows, width = tok.shape
    local = vg.shape[1]
    span = width // STEPS
    ospan = out.shape[1] // OUT_STEPS
    core_peer = me + 1 - 2 * c
    y_peer = (a * 2 + 1 - b) * 2 + c

    def device(a_at):
        return (a_at * 2 + b) * 2 + c

    def other(nth):
        down = jnp.where(a == 0, 1 + nth, lax.rem(a + line - 1 - nth, line))
        up = jnp.where(a == line - 1, line - 2 - nth, lax.rem(a + 1 + nth, line))
        return jnp.where(odd == 0, down, up)

    def outward(a_at):
        return jnp.where(odd == 0, a_at > a, a_at < a)

    def inward(a_at):
        return jnp.where(odd == 0, a_at < a, a_at > a)

    def send(src, dst, ssem, rsem, to):
        pltpu.make_async_remote_copy(
            src_ref=src, dst_ref=dst, send_sem=ssem, recv_sem=rsem,
            device_id={"hid": to}, device_id_type=MESH).start()

    def settle(ref, sem):
        pltpu.make_async_copy(ref, ref, sem).wait()

    barrier = pltpu.get_barrier_semaphore()

    def greet(to):
        pl.semaphore_signal(barrier, inc=1, device_id={"hid": to}, device_id_type=MESH)

    greet(core_peer)
    greet(y_peer)
    greet(device(mate))
    for at in range(line):
        @pl.when(inward(at))
        def _():
            greet(device(at))

    inputs = [pltpu.make_async_copy(src, dst, in_sem.at[at])
              for at, (src, dst) in enumerate(((tok_in, tok), (gain_in, gain), (clip_in, clip)))]
    for copy in inputs:
        copy.start()

    at_row = lax.broadcasted_iota(jnp.int32, (BLOCK, BLOCK), 0)
    at_col = lax.broadcasted_iota(jnp.int32, (BLOCK, BLOCK), 1)
    bits = at_row & at_col
    folded = bits
    for place in range(1, (BLOCK - 1).bit_length()):
        folded = folded ^ (bits >> place)
    table[...] = (1 - 2 * (folded & 1)).astype(F32).astype(BF)

    for copy in inputs:
        copy.wait()

    weight_copies = []
    for s in range(STEPS):
        part = pl.ds(s * span, span)
        weight_copies.append((
            pltpu.make_async_copy(wg.at[part, :], vg.at[part, :], wsem.at[s]),
            pltpu.make_async_copy(wu.at[part, :], vu.at[part, :], wsem.at[s])))
        for copy in weight_copies[-1]:
            copy.start()
    pltpu.make_async_copy(wd, vd, dsem).start()


    values = tok[...].astype(F32)
    inverse = lax.rsqrt(jnp.mean(values * values, axis=-1, keepdims=True) + 1e-05)
    x[c, k] = (values * inverse * gain[...]).astype(BF)

    with jax.named_scope("barrier"):
        pl.semaphore_wait(barrier, 2 + line // 2)

    def block(a_at, b_at, s):
        return x.at[c, a_at * 2 + b_at, :, pl.ds(s * span, span)]

    def begin_line(s):
        mine = block(a, b, s)
        for step in range(1, line // 2):
            pair = lax.rem(a // 2 + step, line // 2)
            near = 2 * pair + (pair < a // 2).astype(jnp.int32)
            send(mine, mine, ag_send, z_recv.at[s, a], device(near))
        send(mine, mine, ag_send, z_recv.at[s, a], device(mate))

    def begin_rows(s):
        mine = block(a, b, s)
        send(mine, mine, ag_send, y_recv.at[s, a], y_peer)
        send(mine, mine, core_send, c_recv.at[s], core_peer)

    for s in range(STEPS):
        if s < AHEAD:
            begin_line(s)
        begin_rows(s)

    def relay_line(s, first, last):
        for nth in range(first, last):
            src = other(nth)
            got = block(src, b, s)
            settle(got, z_recv.at[s, src])

            @pl.when(inward(src))
            def _():
                send(got, got, relay_send, z_recv.at[s, src], device(mate))
            send(got, got, ag_send, y_recv.at[s, src], y_peer)
            send(got, got, core_send, c_recv.at[s], core_peer)

    def relay_rows(s):
        for nth in range(line):
            src = a if nth == 0 else other(nth - 1)
            got = block(src, 1 - b, s)
            settle(got, y_recv.at[s, src])
            send(got, got, core_send, c_recv.at[s], core_peer)

    def project(s):
        part = pl.ds(s * span, span)
        with jax.named_scope("pwait"):
            settle(x.at[1 - c, :, :, part], c_recv.at[s])
        with jax.named_scope("wwait"):
            settle(vg.at[pl.ds(0, 2 * span), :], wsem.at[s])
        left = x[:, :, :, part].reshape(n * rows, span)
        for acc, weight in ((gate, vg), (up, vu)):
            term = jnp.dot(left, weight[part, :], preferred_element_type=F32)
            acc[...] = term if s == 0 else acc[...] + term

    outer = (a == 0) | (a == line - 1)

    @pl.when(outer)
    def _():
        for s in range(STEPS):
            with jax.named_scope(f"relay_first{s}"):
                relay_line(s, 0, 1)

    inner = jnp.logical_not(outer)
    for s in range(STEPS + BEHIND + 1):
        if s < STEPS:
            with jax.named_scope(f"relay_line{s}"):
                if s <= BEHIND:
                    @pl.when(inner)
                    def _():
                        relay_line(s, 0, 1)
                    relay_line(s, 1, line - 1)
                else:
                    @pl.when(outer)
                    def _():
                        relay_line(s, 1, line - 1)
        if s == BEHIND:
            @pl.when(inner)
            def _():
                for later in range(BEHIND + 1, STEPS):
                    relay_line(later, 0, line - 1)
        if 0 <= s - BEHIND < STEPS:
            with jax.named_scope(f"relay_rows{s-BEHIND}"):
                relay_rows(s - BEHIND)
        if 0 <= s - BEHIND - 1 < STEPS:
            with jax.named_scope(f"project{s-BEHIND-1}"):
                project(s - BEHIND - 1)

    half = chips * rows
    for h in range(2):
        with jax.named_scope(f"swiglu{h}"):
            group = pl.ds(h * half, half)
            for at in range(local // BLOCK):
                tile = pl.ds(at * BLOCK, BLOCK)
                value = gate[group, tile]
                hidden = value / (1.0 + jnp.exp(-value)) * up[group, tile]
                gate[group, tile] = jnp.dot(hidden.astype(BF), table[...], preferred_element_type=F32)
            for q in range(chips):
                values = gate[pl.ds((h * chips + q) * rows, rows), :]
                turned = walsh([values[:, at * BLOCK:(at + 1) * BLOCK] for at in range(local // BLOCK)])
                hs[h, q] = (turned[0] if len(turned) == 1 else jnp.concatenate(turned, axis=1)).astype(BF)
            for shift in range(1, chips):
                q = lax.rem(k + shift, chips)
                send(hs.at[h, q], hr.at[me], a_send, a_recv, q * 2 + h)

            @pl.when(c == h)
            def _():
                pltpu.make_async_copy(hs.at[h, k], hr.at[me], a_recv).start()

            @pl.when(c != h)
            def _():
                send(hs.at[h, k], hr.at[me], a_send, a_recv, core_peer)

    with jax.named_scope("exch0"):
        settle(hr, a_recv)
    factor = 1.0 / math.sqrt(n * local)
    lanes = 128
    with jax.named_scope("walsh1"):
        for j in range(local // lanes):
            tile = pl.ds(j * lanes, lanes)
            turned = walsh([hr[d, :, tile].astype(F32) for d in range(n)])
            for d in range(n):
                bs[d, :, tile] = (turned[d] * factor).astype(BF)
    with jax.named_scope("exch1"):
        for shift in range(1, n):
            to = lax.rem(me + shift, n)
            send(bs.at[to], br.at[c, k], b_send, b_recv.at[c], to)
        pltpu.make_async_copy(bs.at[me], br.at[c, k], b_recv.at[c]).start()

    limit = 127.0 * clip[...]

    def clipped(h):
        with jax.named_scope(f"cwait{h}"):
            settle(br.at[h], b_recv.at[h])
        for q in range(chips // 2):
            values = jnp.concatenate([br[h, 2 * q].astype(F32), br[h, 2 * q + 1].astype(F32)], axis=0)
            y[h, pl.ds(2 * q * rows, 2 * rows), :] = jnp.clip(values, -limit, limit).astype(BF)

    def down(hs_, t):
        part = pl.ds(pl.multiple_of(t * ospan, ospan), ospan)
        left = y[hs_[0]] if len(hs_) == 1 else y[...].reshape(2 * half, local)
        result = jnp.dot(left, vd[:, part], preferred_element_type=F32)
        if len(hs_) == 1:
            own[hs_[0], t] = result.reshape(chips, rows, ospan)
        else:
            own[:, t] = result.reshape(2, chips, rows, ospan)

        def share():
            cs[t] = own[1 - c, t].astype(BF)
            send(cs.at[t], cr.at[t], rs_send.at[0], rc_recv.at[t], core_peer)

        if len(hs_) == 1:
            pl.when(c != hs_[0])(share)
        else:
            share()

    def order(at):
        return lax.rem(at + HEAD * c, OUT_STEPS)

    def over_rows(nth_step):
        t = order(nth_step)
        settle(cr.at[t], rc_recv.at[t])
        for nth in range(line):
            at = lax.rem(a + nth, line) * 2 + 1 - b
            ys[t, nth] = (own[c, t, at] + cr[t, at].astype(F32)).astype(BF)
        far = pl.ds(1, line - 1)
        send(ys.at[t, far], yr.at[t, far], rs_send.at[1], y_recv.at[t, 1], y_peer)

    def own_rows():
        for at in range(TURNED, OUT_STEPS):
            t = order(at)
            send(ys.at[t, 0], yr.at[t, 0], rs_send.at[1], y_recv.at[t, 0], y_peer)

    def column(t, at):
        landed = yr[t, lax.rem(at - a + line, line)].astype(F32)
        return own[c, t, at * 2 + b] + cr[t, at * 2 + b].astype(F32) + landed

    def to_mate(nth_step):
        t = order(nth_step)
        settle(yr.at[t, pl.ds(1, line - 1)], y_recv.at[t, 1])
        for at in range(line):
            @pl.when(outward(at))
            def _():
                zs[t, at] = column(t, at).astype(BF)
                send(zs.at[t, at], zr.at[t, at], rs_send.at[2], rz_recv.at[t, at], device(mate))

    def to_line(nth_step):
        t = order(nth_step)
        for at in range(line):
            @pl.when(inward(at))
            def _():
                settle(zr.at[t, at], rz_recv.at[t, at])
                zs[t, at] = (column(t, at) + zr[t, at].astype(F32)).astype(BF)
                send(zs.at[t, at], pr.at[t, a // 2], rs_send.at[2], y_recv.at[t, 2 + a // 2], device(at))

    def finish(nth_step):
        t = order(nth_step)
        settle(yr.at[t, 0], y_recv.at[t, 0])
        settle(zr.at[t, a], rz_recv.at[t, a])
        values = column(t, a) + zr[t, a].astype(F32)
        for step in range(1, line // 2):
            pair = lax.rem(a // 2 + step, line // 2)
            settle(pr.at[t, pair], y_recv.at[t, 2 + pair])
            values = values + pr[t, pair].astype(F32)
        part = pl.ds(pl.multiple_of(t * ospan, ospan), ospan)
        out[:, part] = (tok[:, part].astype(F32) + values).astype(out.dtype)

    def turned_mate(i):
        t = order(i)
        settle(cr.at[t], rc_recv.at[t])
        for at in range(line):
            @pl.when(outward(at))
            def _():
                for b_at in range(2):
                    q = at * 2 + b_at
                    zs2[i, at, b_at] = (own[c, t, q] + cr[t, q].astype(F32)).astype(BF)
                send(zs2.at[i, at], zr2.at[i, at], rs_send.at[3], sz_recv.at[i, at], device(mate))

    def turned_line(i):
        t = order(i)
        for at in range(line):
            @pl.when(inward(at))
            def _():
                settle(zr2.at[i, at], sz_recv.at[i, at])
                for b_at in range(2):
                    q = at * 2 + b_at
                    zs2[i, at, b_at] = (own[c, t, q] + cr[t, q].astype(F32) + zr2[i, at, b_at].astype(F32)).astype(BF)
                send(zs2.at[i, at], pr2.at[i, a // 2], rs_send.at[3], sp_recv.at[i, a // 2], device(at))

    def line_sum(i, b_at):
        t = order(i)
        q = a * 2 + b_at
        values = own[c, t, q] + cr[t, q].astype(F32) + zr2[i, a, b_at].astype(F32)
        for step in range(1, line // 2):
            pair = lax.rem(a // 2 + step, line // 2)
            values = values + pr2[i, pair, b_at].astype(F32)
        return values

    def turned_rows(i):
        settle(zr2.at[i, a], sz_recv.at[i, a])
        for step in range(1, line // 2):
            pair = lax.rem(a // 2 + step, line // 2)
            settle(pr2.at[i, pair], sp_recv.at[i, pair])
        yo[i] = line_sum(i, 1 - b).astype(BF)
        send(yo.at[i], yi.at[i], rs_send.at[4], sy_recv.at[i], y_peer)

    def turned_finish(i):
        settle(yi.at[i], sy_recv.at[i])
        part = pl.ds(pl.multiple_of(order(i) * ospan, ospan), ospan)
        out[:, part] = (tok[:, part].astype(F32) + line_sum(i, b) + yi[i].astype(F32)).astype(out.dtype)

    table_of_stages = (
        [(lag, stage, 0, TURNED) for lag, stage in zip(TURNED_LAG, (turned_mate, turned_line, turned_rows, turned_finish))]
        + [(lag, stage, TURNED, OUT_STEPS) for lag, stage in zip(LAG, (over_rows, to_mate, to_line, finish))])

    def stages(u):
        @pl.when(u == LATE[0] + (LATE[1] - LATE[0]) * c)
        def _():
            own_rows()

        for (first, last), stage, low, high in table_of_stages:
            i = u - first - (last - first) * c

            @pl.when((i >= low) & (i < high))
            def _():
                with jax.named_scope(stage.__name__):
                    stage(i)

    def run(hs_, start, count, base=0):
        @pl.loop(0, count)
        def _(i):
            if hs_:
                with jax.named_scope("down"):
                    down(hs_, base + i)
            stages(start + i)

    clipped(0)
    pltpu.make_async_copy(wd, vd, dsem).wait()
    run((0,), 0, HEAD)
    clipped(1)
    run((0, 1), HEAD, OUT_STEPS - HEAD, HEAD)
    run((1,), OUT_STEPS, HEAD)
    run((), OUT_STEPS + HEAD, LAG[-1][1] - HEAD)

    with jax.named_scope("drain"):
        for copies in range(1, line):
            @pl.when(jnp.where(odd == 0, a, line - 1 - a) == copies)
            def _():
                settle(x.at[0, pl.ds(0, copies)], relay_send)
        settle(x.at[0], core_send)
        settle(x.at[0, pl.ds(0, line + line // 2)], ag_send)
        settle(hr.at[pl.ds(0, n - 1)], a_send)
        settle(hr.at[pl.ds(0, n - 1)], b_send)
        settle(cs, rs_send.at[0])
        settle(ys.at[pl.ds(0, OUT_STEPS - TURNED)], rs_send.at[1])
        settle(zs.at[pl.ds(0, OUT_STEPS - TURNED), pl.ds(0, line - 1)], rs_send.at[2])
        settle(zs2.at[:, pl.ds(0, line - 1)], rs_send.at[3])
        settle(yo, rs_send.at[4])


def layer(n, tokens, norm_gain, gate_weight, up_weight, down_weight, clip_scale):
    rows, width = tokens.shape
    local = gate_weight.shape[1]
    outs = down_weight.shape[1]
    line, chips = n // 4, n // 2
    total = n * rows
    ospan = outs // OUT_STEPS
    steps = max(STEPS, OUT_STEPS)
    vmem = pl.BlockSpec(memory_space=pltpu.VMEM)
    hbm = pl.BlockSpec(memory_space=pl.ANY)
    dma = pltpu.SemaphoreType.DMA
    return pl.pallas_call(
        functools.partial(kernel, n),
        out_shape=pltpu.VMEM((rows, outs), BF),
        in_specs=[hbm, hbm, hbm, hbm, hbm, hbm],
        out_specs=vmem,
        scratch_shapes=[
            pltpu.VMEM((rows, width), BF),
            pltpu.VMEM((1, width), F32),
            pltpu.VMEM((1, local), F32),
            pltpu.VMEM((2, chips, rows, width), BF),
            pltpu.VMEM((width, local), BF),
            pltpu.VMEM((width, local), BF),
            pltpu.VMEM((local, outs), BF),
            pltpu.VMEM((total, local), F32),
            pltpu.VMEM((total, local), F32),
            pltpu.VMEM((BLOCK, BLOCK), BF),
            pltpu.VMEM((2, chips, rows, local), BF),
            pltpu.VMEM((n, rows, local), BF),
            pltpu.VMEM((n, rows, local), BF),
            pltpu.VMEM((2, chips, rows, local), BF),
            pltpu.VMEM((2, chips * rows, local), BF),
            pltpu.VMEM((2, OUT_STEPS, chips, rows, ospan), F32),
            pltpu.VMEM((OUT_STEPS, chips, rows, ospan), BF),
            pltpu.VMEM((OUT_STEPS, chips, rows, ospan), BF),
            pltpu.VMEM((OUT_STEPS, line, rows, ospan), BF),
            pltpu.VMEM((OUT_STEPS, line, rows, ospan), BF),
            pltpu.VMEM((OUT_STEPS, line, rows, ospan), BF),
            pltpu.VMEM((OUT_STEPS, line, rows, ospan), BF),
            pltpu.VMEM((OUT_STEPS, line // 2, rows, ospan), BF),
            pltpu.VMEM((TURNED, line, 2, rows, ospan), BF),
            pltpu.VMEM((TURNED, line, 2, rows, ospan), BF),
            pltpu.VMEM((TURNED, line // 2, 2, rows, ospan), BF),
            pltpu.VMEM((TURNED, rows, ospan), BF),
            pltpu.VMEM((TURNED, rows, ospan), BF),
            dma((3,)), dma((STEPS,)), dma(()), dma(()), dma(()), dma(()),
            dma((steps, line)), dma((steps, line)), dma((steps,)),
            dma(()), dma(()), dma(()), dma((2,)), dma((5,)),
            dma((TURNED, line)), dma((TURNED, line // 2)), dma((TURNED,)),
        ],
        compiler_params=pltpu.CompilerParams(
            collective_id=0, has_side_effects=True, vmem_limit_bytes=66000000),
    )(tokens, norm_gain.reshape(1, -1), gate_weight, up_weight, down_weight, clip_scale.reshape(1, -1))


def solution(mesh):
    in_specs = (
        P(("groups", "hid"), None),
        P(),
        P(None, "hid"),
        P(None, "hid"),
        P("hid", None),
        P("hid"),
    )
    return jax.shard_map(
        functools.partial(layer, mesh.shape["hid"]), mesh=mesh, in_specs=in_specs,
        out_specs=P(("groups", "hid"), None), check_vma=False)
```

```python
import functools
import math

import jax
import jax.numpy as jnp
from jax import lax
from jax.experimental import pallas as pl
from jax.experimental.pallas import tpu as pltpu
from jax.sharding import PartitionSpec as P

BLOCK = 256
STEPS = 8
OUT_STEPS = 8
AHEAD = 8
BEHIND = 4
HEAD = 4
TURNED = 1
LAG = ((2, 6), (8, 14), (10, 16), (18, 24))
TURNED_LAG = ((2, 6), (7, 11), (13, 17), (18, 24))
LATE = (15, 14)
MESH = pl.DeviceIdType.MESH
BF = jnp.bfloat16
F32 = jnp.float32


def walsh(parts):
    parts = list(parts)
    half = 1
    while half < len(parts):
        for at in range(len(parts)):
            if at & half == 0:
                low, high = parts[at], parts[at + half]
                parts[at], parts[at + half] = low + high, low - high
        half *= 2
    return parts


def kernel(n, tok_in, gain_in, wg, wu, wd, clip_in, out,
           tok, gain, clip, x, vg, vu, vd, gate, up, table, hs, hr, bs, br, y,
           own, cs, cr, ys, yr, zs, zr, pr, zs2, zr2, pr2, yo, yi,
           in_sem, wsem, dsem, ag_send, core_send, relay_send, z_recv, y_recv, c_recv,
           a_send, b_send, a_recv, b_recv, rs_send, sz_recv, sp_recv, sy_recv):
    rc_recv, rz_recv = c_recv, z_recv
    me = lax.axis_index("hid")
    line, chips = n // 4, n // 2
    a, b, c = me // 4, (me // 2) % 2, me % 2
    k = me // 2
    odd = a % 2
    mate = a + 1 - 2 * odd
    rows, width = tok.shape
    local = vg.shape[1]
    span = width // STEPS
    ospan = out.shape[1] // OUT_STEPS
    core_peer = me + 1 - 2 * c
    y_peer = (a * 2 + 1 - b) * 2 + c

    def device(a_at):
        return (a_at * 2 + b) * 2 + c

    def other(nth):
        down = jnp.where(a == 0, 1 + nth, lax.rem(a + line - 1 - nth, line))
        up = jnp.where(a == line - 1, line - 2 - nth, lax.rem(a + 1 + nth, line))
        return jnp.where(odd == 0, down, up)

    def outward(a_at):
        return jnp.where(odd == 0, a_at > a, a_at < a)

    def inward(a_at):
        return jnp.where(odd == 0, a_at < a, a_at > a)

    def send(src, dst, ssem, rsem, to):
        pltpu.make_async_remote_copy(
            src_ref=src, dst_ref=dst, send_sem=ssem, recv_sem=rsem,
            device_id={"hid": to}, device_id_type=MESH).start()

    def settle(ref, sem):
        pltpu.make_async_copy(ref, ref, sem).wait()

    barrier = pltpu.get_barrier_semaphore()

    def greet(to):
        pl.semaphore_signal(barrier, inc=1, device_id={"hid": to}, device_id_type=MESH)

    greet(core_peer)
    greet(y_peer)
    greet(device(mate))
    for at in range(line):
        @pl.when(inward(at))
        def _():
            greet(device(at))

    inputs = [pltpu.make_async_copy(src, dst, in_sem.at[at])
              for at, (src, dst) in enumerate(((tok_in, tok), (gain_in, gain), (clip_in, clip)))]
    for copy in inputs:
        copy.start()

    at_row = lax.broadcasted_iota(jnp.int32, (BLOCK, BLOCK), 0)
    at_col = lax.broadcasted_iota(jnp.int32, (BLOCK, BLOCK), 1)
    bits = at_row & at_col
    folded = bits
    for place in range(1, (BLOCK - 1).bit_length()):
        folded = folded ^ (bits >> place)
    table[...] = (1 - 2 * (folded & 1)).astype(F32).astype(BF)

    for copy in inputs:
        copy.wait()

    weight_copies = []
    for s in range(STEPS):
        part = pl.ds(s * span, span)
        weight_copies.append((
            pltpu.make_async_copy(wg.at[part, :], vg.at[part, :], wsem.at[s]),
            pltpu.make_async_copy(wu.at[part, :], vu.at[part, :], wsem.at[s])))
        for copy in weight_copies[-1]:
            copy.start()
    pltpu.make_async_copy(wd, vd, dsem).start()


    values = tok[...].astype(F32)
    inverse = lax.rsqrt(jnp.mean(values * values, axis=-1, keepdims=True) + 1e-05)
    x[c, k] = (values * inverse * gain[...]).astype(BF)

    with jax.named_scope("barrier"):
        pl.semaphore_wait(barrier, 2 + line // 2)

    def block(a_at, b_at, s):
        return x.at[c, a_at * 2 + b_at, :, pl.ds(s * span, span)]

    def begin_line(s):
        mine = block(a, b, s)
        for step in range(1, line // 2):
            pair = lax.rem(a // 2 + step, line // 2)
            near = 2 * pair + (pair < a // 2).astype(jnp.int32)
            send(mine, mine, ag_send, z_recv.at[s, a], device(near))
        send(mine, mine, ag_send, z_recv.at[s, a], device(mate))

    def begin_rows(s):
        mine = block(a, b, s)
        send(mine, mine, ag_send, y_recv.at[s, a], y_peer)
        send(mine, mine, core_send, c_recv.at[s], core_peer)

    for s in range(STEPS):
        if s < AHEAD:
            begin_line(s)
        begin_rows(s)

    def relay_line(s, first, last):
        for nth in range(first, last):
            src = other(nth)
            got = block(src, b, s)
            settle(got, z_recv.at[s, src])

            @pl.when(inward(src))
            def _():
                send(got, got, relay_send, z_recv.at[s, src], device(mate))
            send(got, got, ag_send, y_recv.at[s, src], y_peer)
            send(got, got, core_send, c_recv.at[s], core_peer)

    def relay_rows(s):
        for nth in range(line):
            src = a if nth == 0 else other(nth - 1)
            got = block(src, 1 - b, s)
            settle(got, y_recv.at[s, src])
            send(got, got, core_send, c_recv.at[s], core_peer)

    def project(s):
        part = pl.ds(s * span, span)
        with jax.named_scope("pwait"):
            settle(x.at[1 - c, :, :, part], c_recv.at[s])
        with jax.named_scope("wwait"):
            settle(vg.at[pl.ds(0, 2 * span), :], wsem.at[s])
        left = x[:, :, :, part].reshape(n * rows, span)
        for acc, weight in ((gate, vg), (up, vu)):
            term = jnp.dot(left, weight[part, :], preferred_element_type=F32)
            acc[...] = term if s == 0 else acc[...] + term

    outer = (a == 0) | (a == line - 1)

    @pl.when(outer)
    def _():
        for s in range(STEPS):
            with jax.named_scope(f"relay_first{s}"):
                relay_line(s, 0, 1)

    inner = jnp.logical_not(outer)
    late = outer & (c == 0)
    for s in range(STEPS + BEHIND + 1):
        if s < STEPS:
            with jax.named_scope(f"relay_line{s}"):
                if s <= BEHIND:
                    @pl.when(inner)
                    def _():
                        relay_line(s, 0, 1)
                    relay_line(s, 1, line - 1)
                else:
                    @pl.when(late)
                    def _():
                        relay_line(s, 1, line - 1)
        if s == BEHIND:
            @pl.when(jnp.logical_not(late))
            def _():
                for later in range(BEHIND + 1, STEPS):
                    @pl.when(inner)
                    def _():
                        relay_line(later, 0, 1)
                    relay_line(later, 1, line - 1)
        if 0 <= s - BEHIND < STEPS:
            with jax.named_scope(f"relay_rows{s-BEHIND}"):
                relay_rows(s - BEHIND)
        if 0 <= s - BEHIND - 1 < STEPS:
            with jax.named_scope(f"project{s-BEHIND-1}"):
                project(s - BEHIND - 1)

    half = chips * rows
    for h in range(2):
        with jax.named_scope(f"swiglu{h}"):
            group = pl.ds(h * half, half)
            for at in range(local // BLOCK):
                tile = pl.ds(at * BLOCK, BLOCK)
                value = gate[group, tile]
                hidden = value / (1.0 + jnp.exp(-value)) * up[group, tile]
                gate[group, tile] = jnp.dot(hidden.astype(BF), table[...], preferred_element_type=F32)
            for q in range(chips):
                values = gate[pl.ds((h * chips + q) * rows, rows), :]
                turned = walsh([values[:, at * BLOCK:(at + 1) * BLOCK] for at in range(local // BLOCK)])
                hs[h, q] = (turned[0] if len(turned) == 1 else jnp.concatenate(turned, axis=1)).astype(BF)
            for shift in range(1, chips):
                q = lax.rem(k + shift, chips)
                send(hs.at[h, q], hr.at[me], a_send, a_recv, q * 2 + h)

            @pl.when(c == h)
            def _():
                pltpu.make_async_copy(hs.at[h, k], hr.at[me], a_recv).start()

            @pl.when(c != h)
            def _():
                send(hs.at[h, k], hr.at[me], a_send, a_recv, core_peer)

    with jax.named_scope("exch0"):
        settle(hr, a_recv)
    factor = 1.0 / math.sqrt(n * local)
    lanes = 128
    with jax.named_scope("walsh1"):
        for j in range(local // lanes):
            tile = pl.ds(j * lanes, lanes)
            turned = walsh([hr[d, :, tile].astype(F32) for d in range(n)])
            for d in range(n):
                bs[d, :, tile] = (turned[d] * factor).astype(BF)
    with jax.named_scope("exch1"):
        for shift in range(1, n):
            to = lax.rem(me + shift, n)
            send(bs.at[to], br.at[c, k], b_send, b_recv.at[c], to)
        pltpu.make_async_copy(bs.at[me], br.at[c, k], b_recv.at[c]).start()

    limit = 127.0 * clip[...]

    def clipped(h):
        with jax.named_scope(f"cwait{h}"):
            settle(br.at[h], b_recv.at[h])
        for q in range(chips // 2):
            values = jnp.concatenate([br[h, 2 * q].astype(F32), br[h, 2 * q + 1].astype(F32)], axis=0)
            y[h, pl.ds(2 * q * rows, 2 * rows), :] = jnp.clip(values, -limit, limit).astype(BF)

    def down(hs_, t):
        part = pl.ds(pl.multiple_of(t * ospan, ospan), ospan)
        left = y[hs_[0]] if len(hs_) == 1 else y[...].reshape(2 * half, local)
        result = jnp.dot(left, vd[:, part], preferred_element_type=F32)
        if len(hs_) == 1:
            own[hs_[0], t] = result.reshape(chips, rows, ospan)
        else:
            own[:, t] = result.reshape(2, chips, rows, ospan)

        def share():
            cs[t] = own[1 - c, t].astype(BF)
            send(cs.at[t], cr.at[t], rs_send.at[0], rc_recv.at[t], core_peer)

        if len(hs_) == 1:
            pl.when(c != hs_[0])(share)
        else:
            share()

    def order(at):
        return lax.rem(at + HEAD * c, OUT_STEPS)

    def over_rows(nth_step):
        t = order(nth_step)
        settle(cr.at[t], rc_recv.at[t])
        for nth in range(line):
            at = lax.rem(a + nth, line) * 2 + 1 - b
            ys[t, nth] = (own[c, t, at] + cr[t, at].astype(F32)).astype(BF)
        far = pl.ds(1, line - 1)
        send(ys.at[t, far], yr.at[t, far], rs_send.at[1], y_recv.at[t, 1], y_peer)

    def own_rows():
        for at in range(TURNED, OUT_STEPS):
            t = order(at)
            send(ys.at[t, 0], yr.at[t, 0], rs_send.at[1], y_recv.at[t, 0], y_peer)

    def column(t, at):
        landed = yr[t, lax.rem(at - a + line, line)].astype(F32)
        return own[c, t, at * 2 + b] + cr[t, at * 2 + b].astype(F32) + landed

    def to_mate(nth_step):
        t = order(nth_step)
        settle(yr.at[t, pl.ds(1, line - 1)], y_recv.at[t, 1])
        for at in range(line):
            @pl.when(outward(at))
            def _():
                zs[t, at] = column(t, at).astype(BF)
                send(zs.at[t, at], zr.at[t, at], rs_send.at[2], rz_recv.at[t, at], device(mate))

    def to_line(nth_step):
        t = order(nth_step)
        for at in range(line):
            @pl.when(inward(at))
            def _():
                settle(zr.at[t, at], rz_recv.at[t, at])
                zs[t, at] = (column(t, at) + zr[t, at].astype(F32)).astype(BF)
                send(zs.at[t, at], pr.at[t, a // 2], rs_send.at[2], y_recv.at[t, 2 + a // 2], device(at))

    def finish(nth_step):
        t = order(nth_step)
        settle(yr.at[t, 0], y_recv.at[t, 0])
        settle(zr.at[t, a], rz_recv.at[t, a])
        values = column(t, a) + zr[t, a].astype(F32)
        for step in range(1, line // 2):
            pair = lax.rem(a // 2 + step, line // 2)
            settle(pr.at[t, pair], y_recv.at[t, 2 + pair])
            values = values + pr[t, pair].astype(F32)
        part = pl.ds(pl.multiple_of(t * ospan, ospan), ospan)
        out[:, part] = (tok[:, part].astype(F32) + values).astype(out.dtype)

    def turned_mate(i):
        t = order(i)
        settle(cr.at[t], rc_recv.at[t])
        for at in range(line):
            @pl.when(outward(at))
            def _():
                for b_at in range(2):
                    q = at * 2 + b_at
                    zs2[i, at, b_at] = (own[c, t, q] + cr[t, q].astype(F32)).astype(BF)
                send(zs2.at[i, at], zr2.at[i, at], rs_send.at[3], sz_recv.at[i, at], device(mate))

    def turned_line(i):
        t = order(i)
        for at in range(line):
            @pl.when(inward(at))
            def _():
                settle(zr2.at[i, at], sz_recv.at[i, at])
                for b_at in range(2):
                    q = at * 2 + b_at
                    zs2[i, at, b_at] = (own[c, t, q] + cr[t, q].astype(F32) + zr2[i, at, b_at].astype(F32)).astype(BF)
                send(zs2.at[i, at], pr2.at[i, a // 2], rs_send.at[3], sp_recv.at[i, a // 2], device(at))

    def line_sum(i, b_at):
        t = order(i)
        q = a * 2 + b_at
        values = own[c, t, q] + cr[t, q].astype(F32) + zr2[i, a, b_at].astype(F32)
        for step in range(1, line // 2):
            pair = lax.rem(a // 2 + step, line // 2)
            values = values + pr2[i, pair, b_at].astype(F32)
        return values

    def turned_rows(i):
        settle(zr2.at[i, a], sz_recv.at[i, a])
        for step in range(1, line // 2):
            pair = lax.rem(a // 2 + step, line // 2)
            settle(pr2.at[i, pair], sp_recv.at[i, pair])
        yo[i] = line_sum(i, 1 - b).astype(BF)
        send(yo.at[i], yi.at[i], rs_send.at[4], sy_recv.at[i], y_peer)

    def turned_finish(i):
        settle(yi.at[i], sy_recv.at[i])
        part = pl.ds(pl.multiple_of(order(i) * ospan, ospan), ospan)
        out[:, part] = (tok[:, part].astype(F32) + line_sum(i, b) + yi[i].astype(F32)).astype(out.dtype)

    table_of_stages = (
        [(lag, stage, 0, TURNED) for lag, stage in zip(TURNED_LAG, (turned_mate, turned_line, turned_rows, turned_finish))]
        + [(lag, stage, TURNED, OUT_STEPS) for lag, stage in zip(LAG, (over_rows, to_mate, to_line, finish))])

    def stages(u):
        @pl.when(u == LATE[0] + (LATE[1] - LATE[0]) * c)
        def _():
            own_rows()

        for (first, last), stage, low, high in table_of_stages:
            i = u - first - (last - first) * c

            @pl.when((i >= low) & (i < high))
            def _():
                with jax.named_scope(stage.__name__):
                    stage(i)

    def run(hs_, start, count, base=0):
        @pl.loop(0, count)
        def _(i):
            if hs_:
                with jax.named_scope("down"):
                    down(hs_, base + i)
            stages(start + i)

    clipped(0)
    pltpu.make_async_copy(wd, vd, dsem).wait()
    run((0,), 0, HEAD)
    clipped(1)
    run((0, 1), HEAD, OUT_STEPS - HEAD, HEAD)
    run((1,), OUT_STEPS, HEAD)
    run((), OUT_STEPS + HEAD, LAG[-1][1] - HEAD)

    with jax.named_scope("drain"):
        for copies in range(1, line):
            @pl.when(jnp.where(odd == 0, a, line - 1 - a) == copies)
            def _():
                settle(x.at[0, pl.ds(0, copies)], relay_send)
        settle(x.at[0], core_send)
        settle(x.at[0, pl.ds(0, line + line // 2)], ag_send)
        settle(hr.at[pl.ds(0, n - 1)], a_send)
        settle(hr.at[pl.ds(0, n - 1)], b_send)
        settle(cs, rs_send.at[0])
        settle(ys.at[pl.ds(0, OUT_STEPS - TURNED)], rs_send.at[1])
        settle(zs.at[pl.ds(0, OUT_STEPS - TURNED), pl.ds(0, line - 1)], rs_send.at[2])
        settle(zs2.at[:, pl.ds(0, line - 1)], rs_send.at[3])
        settle(yo, rs_send.at[4])


def layer(n, tokens, norm_gain, gate_weight, up_weight, down_weight, clip_scale):
    rows, width = tokens.shape
    local = gate_weight.shape[1]
    outs = down_weight.shape[1]
    line, chips = n // 4, n // 2
    total = n * rows
    ospan = outs // OUT_STEPS
    steps = max(STEPS, OUT_STEPS)
    vmem = pl.BlockSpec(memory_space=pltpu.VMEM)
    hbm = pl.BlockSpec(memory_space=pl.ANY)
    dma = pltpu.SemaphoreType.DMA
    return pl.pallas_call(
        functools.partial(kernel, n),
        out_shape=pltpu.VMEM((rows, outs), BF),
        in_specs=[hbm, hbm, hbm, hbm, hbm, hbm],
        out_specs=vmem,
        scratch_shapes=[
            pltpu.VMEM((rows, width), BF),
            pltpu.VMEM((1, width), F32),
            pltpu.VMEM((1, local), F32),
            pltpu.VMEM((2, chips, rows, width), BF),
            pltpu.VMEM((width, local), BF),
            pltpu.VMEM((width, local), BF),
            pltpu.VMEM((local, outs), BF),
            pltpu.VMEM((total, local), F32),
            pltpu.VMEM((total, local), F32),
            pltpu.VMEM((BLOCK, BLOCK), BF),
            pltpu.VMEM((2, chips, rows, local), BF),
            pltpu.VMEM((n, rows, local), BF),
            pltpu.VMEM((n, rows, local), BF),
            pltpu.VMEM((2, chips, rows, local), BF),
            pltpu.VMEM((2, chips * rows, local), BF),
            pltpu.VMEM((2, OUT_STEPS, chips, rows, ospan), F32),
            pltpu.VMEM((OUT_STEPS, chips, rows, ospan), BF),
            pltpu.VMEM((OUT_STEPS, chips, rows, ospan), BF),
            pltpu.VMEM((OUT_STEPS, line, rows, ospan), BF),
            pltpu.VMEM((OUT_STEPS, line, rows, ospan), BF),
            pltpu.VMEM((OUT_STEPS, line, rows, ospan), BF),
            pltpu.VMEM((OUT_STEPS, line, rows, ospan), BF),
            pltpu.VMEM((OUT_STEPS, line // 2, rows, ospan), BF),
            pltpu.VMEM((TURNED, line, 2, rows, ospan), BF),
            pltpu.VMEM((TURNED, line, 2, rows, ospan), BF),
            pltpu.VMEM((TURNED, line // 2, 2, rows, ospan), BF),
            pltpu.VMEM((TURNED, rows, ospan), BF),
            pltpu.VMEM((TURNED, rows, ospan), BF),
            dma((3,)), dma((STEPS,)), dma(()), dma(()), dma(()), dma(()),
            dma((steps, line)), dma((steps, line)), dma((steps,)),
            dma(()), dma(()), dma(()), dma((2,)), dma((5,)),
            dma((TURNED, line)), dma((TURNED, line // 2)), dma((TURNED,)),
        ],
        compiler_params=pltpu.CompilerParams(
            collective_id=0, has_side_effects=True, vmem_limit_bytes=66000000),
    )(tokens, norm_gain.reshape(1, -1), gate_weight, up_weight, down_weight, clip_scale.reshape(1, -1))


def solution(mesh):
    in_specs = (
        P(("groups", "hid"), None),
        P(),
        P(None, "hid"),
        P(None, "hid"),
        P("hid", None),
        P("hid"),
    )
    return jax.shard_map(
        functools.partial(layer, mesh.shape["hid"]), mesh=mesh, in_specs=in_specs,
        out_specs=P(("groups", "hid"), None), check_vma=False)
```
